32 devices in a mesh: rows: 4 (over y, core), cols: 8 (over z, x).
Axes of the slice: x: 2, y: 2, z: 4, core: 2. Of those that a mesh axis runs over, the one named last changes fastest.
Arguments:
- image: bfloat16 [128, 512, 128], P('rows', 'cols'), may hold values from -6 to 6
- routes: int32 [16, 64, 4], P('rows', 'cols'), may hold values from 0 to 1023, as said below
- norm_gain: float32 [128], replicated, may hold values from 0.1 to 1.9
- qkv_weight: bfloat16 [128, 384], replicated, may hold values from -25.455844 to 25.455844
- lce_weight: float32 [5, 5, 128], replicated, may hold values from -1.25 to 1.25
- out_weight: bfloat16 [128, 128], replicated, may hold values from -0.5 to 0.5
- mlp_gain: float32 [128], replicated, may hold values from 0.1 to 1.9
- up_weight: bfloat16 [128, 384], replicated, may hold values from -0.5 to 0.5
- down_weight: bfloat16 [384, 128], replicated, may hold values from -0.3125 to 0.3125
Outputs:
- refined: bfloat16 [128, 512, 128], P('rows', 'cols')
The draws below stay inside these ranges and needn't reach their ends.
Inputs may be any that keep to these rules, and one draw needn't show every extreme that they name: Each region names 4 different regions. Of the routes of the regions of one device, at most 8 lead to the regions of any one device, and in every draw some device receives exactly 8 from every device.
All inputs are finite; a program needn't handle non-finite values.
Results may differ from the reference program's by a relative error of at most 0.0038.
The reference program's roundings to bfloat16 on the way (of `normed`, `projected`, `weights`, `combined`, `residual`, `second` and `hidden`) count: a program that leaves them out, or rounds other values in their place, can miss the bound.
Values may be sent and summed in bfloat16 or wider, within the bound.
No kernel may reach another device: no remote copies, remote signals or barrier semaphores. Data moves between devices by JAX's collectives and lax.ppermute only.
A program may use at most 128 MiB of HBM per device.

```python
import math
import jax
import jax.numpy as jnp
from jax import lax

C = 128
HEADS = 4
FFN = 384
RS = 8
TOPK = 4
KSIZE = 5
RR = 4
RC = 8
CAP = 8
NRR = 16
NRC = 64
GRID_H = 128
GRID_W = 512


def draw_routes(key, part):
    row_devices = NRR // RR
    col_devices = NRC // RC
    devices = row_devices * col_devices
    region_count = RR * RC
    pair_count = region_count * TOPK
    slot_count = devices * CAP
    base_key = jax.random.fold_in(key, 7)
    hot_key, local_key, jitter_key, sender_keys = jax.random.split(base_key, 4)
    hot_dev = jax.random.randint(hot_key, (), 0, devices)
    hot_local = jax.random.randint(local_key, (devices,), 0, region_count)
    owners = jnp.arange(slot_count, dtype=jnp.int32) // CAP

    def one_sender(sender_key):
        perm_key, order_key = jax.random.split(sender_key)
        ranking = jax.random.permutation(perm_key, slot_count).astype(jnp.int32)
        ranking = ranking - slot_count * (owners == hot_dev).astype(jnp.int32)
        ordered = jnp.argsort(ranking, stable=True)
        chosen = owners[ordered[:pair_count]]
        return chosen[jax.random.permutation(order_key, pair_count)]
    destinations = jax.vmap(one_sender)(jax.random.split(sender_keys, devices))
    destinations = destinations.reshape(devices, region_count, TOPK)
    jitter = jax.random.randint(jitter_key, (devices, region_count, 1), 0, 2)
    picks = jnp.arange(TOPK, dtype=jnp.int32)[None, None, :]
    local_index = (hot_local[destinations] + jitter + picks) % region_count
    region_row = destinations // col_devices * RR + local_index // RC
    region_col = destinations % col_devices * RC + local_index % RC
    global_ids = (region_row * NRC + region_col).astype(jnp.int32)
    shaped = global_ids.reshape(row_devices, col_devices, RR, RC, TOPK)
    return shaped.transpose(0, 2, 1, 3, 4).reshape(NRR, NRC, TOPK)


def draw_qkv_weight(key, part):
    first_key = jax.random.fold_in(jax.random.fold_in(key, 11), 0)
    base_draw = jax.random.truncated_normal(first_key, -3.0, 3.0, (C, 3 * C), jnp.float32) * (1.0 / math.sqrt(C))
    return base_draw.astype(jnp.bfloat16)


def block_scale(own_key, extent, pieces, least, largest):
    gain, own = 1.0, jax.random.fold_in(own_key, 6)
    for axis_at, blocks in pieces:
        heights = jnp.exp(jax.random.uniform(jax.random.fold_in(own, axis_at), (blocks,), jnp.float32, least / len(pieces), largest / len(pieces)))
        gain = gain * jnp.repeat(heights, extent[axis_at] // blocks).reshape([-1 if axis == axis_at else 1 for axis in range(len(extent))])
    return gain


def noise(key, extent, width, most, pieces=(), kind=jnp.bfloat16):
    values = jax.random.normal(key, extent, jnp.float32) * width
    if len(pieces) > 0:
        values = block_scale(key, extent, pieces, -0.22, 0.18) * values
    return jnp.clip(values, min=-most, max=most).astype(kind)


def setup_inputs(seed: int = 0) -> dict:
    key_list = jax.random.split(jax.random.key(seed), 10)
    return {
        "image": noise(key_list[0], (GRID_H, GRID_W, C), 1.0, 6.0, ((0, 4), (1, 8))),
        "routes": draw_routes(jax.random.fold_in(key_list[9], 71), 0),
        "norm_gain": jnp.clip(1.0 + 0.18 * jax.random.normal(key_list[2], (C,), jnp.float32), 0.1, 1.9),
        "qkv_weight": draw_qkv_weight(jax.random.fold_in(key_list[9], 71), 0),
        "lce_weight": noise(key_list[4], (KSIZE, KSIZE, C), (KSIZE * KSIZE) ** -0.5, 1.25, (), jnp.float32),
        "out_weight": noise(key_list[5], (C, C), C ** -0.5, 0.5),
        "mlp_gain": jnp.clip(1.0 + 0.18 * jax.random.normal(key_list[6], (C,), jnp.float32), 0.1, 1.9),
        "up_weight": noise(key_list[7], (C, FFN), C ** -0.5, 0.5),
        "down_weight": noise(key_list[8], (FFN, C), FFN ** -0.5, 0.3125),
    }


EPSILON = 1e-06

def layer_norm(values, norm_scale):
    floats = values.astype(jnp.float32)
    centered = floats - lax.optimization_barrier(jnp.mean(floats, axis=-1, keepdims=True))
    spread = lax.optimization_barrier(jnp.mean(centered * centered, axis=-1, keepdims=True))
    return centered * lax.rsqrt(spread + EPSILON) * norm_scale

def to_regions(grid_field, region_side):
    height, grid_width, channels = grid_field.shape
    shaped = grid_field.reshape(height // region_side, region_side, grid_width // region_side, region_side, channels)
    return shaped.transpose(0, 2, 1, 3, 4).reshape(-1, region_side * region_side, channels)

def from_regions(blocks, region_side, height, grid_width):
    channels = blocks.shape[-1]
    shaped = blocks.reshape(height // region_side, grid_width // region_side, region_side, region_side, channels)
    return shaped.transpose(0, 2, 1, 3, 4).reshape(height, grid_width, channels)

def region_attention(queries, keyvals, head_count):
    group_count, length, channels = queries.shape
    head_size = channels // head_count
    q_heads = queries.astype(jnp.float32).reshape(group_count, length, head_count, head_size)
    k_heads = keyvals[..., :channels].astype(jnp.float32).reshape(group_count, -1, head_count, head_size)
    v_heads = keyvals[..., channels:].astype(jnp.float32).reshape(group_count, -1, head_count, head_size)
    scores = jnp.einsum('gqhd,gkhd->ghqk', q_heads, k_heads) * head_size ** (-0.5)
    row_max = lax.optimization_barrier(jnp.max(scores, axis=-1, keepdims=True))
    expons = jnp.exp(scores - row_max)
    weights = (expons / lax.optimization_barrier(jnp.sum(expons, axis=-1, keepdims=True))).astype(jnp.bfloat16)
    blended = jnp.einsum('ghqk,gkhd->gqhd', weights.astype(jnp.float32), v_heads)
    return blended.reshape(group_count, length, channels)

def local_context(padded, kernel, height, grid_width):
    kernel_size = kernel.shape[0]
    summed = jnp.zeros((height, grid_width, padded.shape[-1]), jnp.float32)
    for offset_row in range(kernel_size):
        for offset_col in range(kernel_size):
            window = padded[offset_row:offset_row + height, offset_col:offset_col + grid_width].astype(jnp.float32)
            summed = summed + window * kernel[offset_row, offset_col].astype(jnp.float32)
    return summed

def reference(image, routes, norm_gain, qkv_weight, lce_weight, out_weight, mlp_gain, up_weight, down_weight):
    height, grid_width, channels = image.shape
    normed = layer_norm(image, norm_gain).astype(jnp.bfloat16)
    projected = jnp.dot(normed.reshape(-1, channels), qkv_weight, preferred_element_type=jnp.float32)
    projected = projected.astype(jnp.bfloat16).reshape(height, grid_width, 3 * channels)
    queries = to_regions(projected[..., :channels], RS)
    keyvals = to_regions(projected[..., channels:], RS)
    values = projected[..., 2 * channels:]
    margin = (lce_weight.shape[0] - 1) // 2
    padded = jnp.pad(values, ((margin, margin), (margin, margin), (0, 0)))
    context = local_context(padded, lce_weight, height, grid_width)
    row_queries = queries.reshape(NRR, NRC, RS * RS, channels)

    def attend(inputs):
        row_block, row_routes = inputs
        chosen = keyvals[row_routes.reshape(-1)].reshape(NRC, TOPK * RS * RS, 2 * channels)
        return region_attention(row_block, chosen, HEADS)
    blended = lax.map(attend, (row_queries, routes))
    attended = from_regions(blended.reshape(NRR * NRC, RS * RS, channels), RS, height, grid_width)
    combined = (attended + context).astype(jnp.bfloat16)
    projected_out = jnp.dot(combined.reshape(-1, channels), out_weight, preferred_element_type=jnp.float32)
    residual = image.astype(jnp.float32) + projected_out.reshape(height, grid_width, channels)
    stored = lax.optimization_barrier(residual.astype(jnp.bfloat16))
    second = layer_norm(stored, mlp_gain).astype(jnp.bfloat16)
    hidden = jax.nn.gelu(jnp.dot(second.reshape(-1, channels), up_weight, preferred_element_type=jnp.float32), approximate=True).astype(jnp.bfloat16)
    lowered = jnp.dot(hidden, down_weight, preferred_element_type=jnp.float32).reshape(height, grid_width, channels)
    return (stored.astype(jnp.float32) + lowered).astype(jnp.bfloat16)
```

```python
import functools
import math

import jax
import jax.numpy as jnp
from jax import lax
from jax.experimental import pallas as pl
from jax.experimental.pallas import tpu as pltpu
from jax.sharding import PartitionSpec as P

HEADS = 4
EPSILON = 1e-06
F32 = jnp.float32
BF16 = jnp.bfloat16


def halo(block, sides, width):
    for axis, dim in sides:
        count = lax.axis_size(axis)
        forward = [(i, i + 1) for i in range(count - 1)]
        backward = [(target, source) for source, target in forward]
        low = lax.ppermute(
            lax.slice_in_dim(block, block.shape[dim] - width, None, axis=dim), axis, forward
        )
        high = lax.ppermute(lax.slice_in_dim(block, 0, width, axis=dim), axis, backward)
        block = jnp.concatenate([low, block, high], axis=dim)
    return block


def normalize(floats, gain):
    centered = floats - jnp.mean(floats, axis=-1, keepdims=True)
    spread = jnp.mean(centered * centered, axis=-1, keepdims=True)
    return centered * lax.rsqrt(spread + EPSILON) * gain


def regions_of(strip, side):
    height, width, channels = strip.shape
    return (
        strip.reshape(height, width // side, side, channels)
        .transpose(1, 0, 2, 3)
        .reshape(height * width, channels)
    )


def strip_of(tokens, side, width):
    channels = tokens.shape[-1]
    return (
        tokens.reshape(width // side, side, side, channels)
        .transpose(1, 0, 2, 3)
        .reshape(side, width, channels)
    )


def norm_kernel(side, image_ref, gain_ref, out_ref):
    normed = normalize(image_ref[...].astype(F32), gain_ref[...])
    out_ref[...] = regions_of(normed, side).astype(BF16).reshape(out_ref.shape)


def norm_regions(image, gain, side):
    height, width, channels = image.shape
    per_row = width // side
    return pl.pallas_call(
        functools.partial(norm_kernel, side),
        grid=(height // side,),
        in_specs=[
            pl.BlockSpec((side, width, channels), lambda i: (i, 0, 0)),
            pl.BlockSpec((1, channels), lambda i: (0, 0)),
        ],
        out_specs=pl.BlockSpec((per_row, side * side, channels), lambda i: (i, 0, 0)),
        out_shape=jax.ShapeDtypeStruct(
            (height // side * per_row, side * side, channels), BF16
        ),
        cost_estimate=pl.CostEstimate(
            flops=10 * image.size, bytes_accessed=4 * image.size, transcendentals=0
        ),
        name="norm_regions",
    )(image, gain.reshape(1, channels))


def context_kernel(side, kernel_size, padded_ref, gain_ref, weight_ref, lce_ref, context_ref, query_ref):
    step = pl.program_id(0)
    rows = side + kernel_size - 1
    channels = padded_ref.shape[-1]
    width = query_ref.shape[0] // side
    strip = padded_ref[pl.ds(step * side, rows)].astype(F32)
    wide = strip.shape[1]
    normed = normalize(strip, gain_ref[...]).astype(BF16).reshape(rows * wide, channels)
    projected = jnp.dot(normed, weight_ref[...], preferred_element_type=F32).astype(BF16)
    values = projected[:, channels:].astype(F32).reshape(rows, wide, channels)
    summed = jnp.zeros((side, width, channels), F32)
    for col in range(kernel_size):
        moved = values if col == 0 else pltpu.roll(values, wide - col, 1)
        moved = moved[:, :width]
        for row in range(kernel_size):
            summed = summed + moved[row : row + side] * lce_ref[row, col]
    context_ref[...] = regions_of(summed, side)
    margin = (kernel_size - 1) // 2
    queries = projected[:, :channels].astype(F32).reshape(rows, wide, channels)
    inner = pltpu.roll(queries, wide - margin, 1)[margin : margin + side, :width]
    query_ref[...] = regions_of(inner, side).astype(BF16)


def context_and_queries(padded, gain, query_value_weight, lce_weight, side, height, width):
    channels = padded.shape[-1]
    kernel_size = lce_weight.shape[0]
    tokens = height * width
    full = lambda shape: pl.BlockSpec(shape, lambda i: (0,) * len(shape))
    return pl.pallas_call(
        functools.partial(context_kernel, side, kernel_size),
        grid=(height // side,),
        in_specs=[
            full(padded.shape),
            full((1, channels)),
            full(query_value_weight.shape),
            full((kernel_size, kernel_size, 1, channels)),
        ],
        out_specs=[
            pl.BlockSpec((side * width, channels), lambda i: (i, 0)),
            pl.BlockSpec((side * width, channels), lambda i: (i, 0)),
        ],
        out_shape=[
            jax.ShapeDtypeStruct((tokens, channels), F32),
            jax.ShapeDtypeStruct((tokens, channels), BF16),
        ],
        cost_estimate=pl.CostEstimate(
            flops=tokens * channels * 600, bytes_accessed=10 * tokens * channels, transcendentals=0
        ),
        name="context",
    )(
        padded,
        gain.reshape(1, channels),
        query_value_weight,
        lce_weight.reshape(kernel_size, kernel_size, 1, channels),
    )


def pack_kernel(index_ref, source_ref, out_ref):
    step = pl.program_id(0)
    count = out_ref.shape[0]

    def one(slot, carry):
        out_ref[slot] = source_ref[index_ref[step * count + slot]]
        return carry

    lax.fori_loop(0, count, one, 0, unroll=True)


def pack(source, index, steps):
    slots = index.shape[0]
    shape = source.shape[1:]
    per_step = slots // steps
    return pl.pallas_call(
        pack_kernel,
        grid_spec=pltpu.PrefetchScalarGridSpec(
            num_scalar_prefetch=1,
            grid=(steps,),
            in_specs=[pl.BlockSpec(source.shape, lambda i, index: (0, 0, 0))],
            out_specs=pl.BlockSpec((per_step, *shape), lambda i, index: (i, 0, 0)),
        ),
        out_shape=jax.ShapeDtypeStruct((slots, *shape), source.dtype),
        cost_estimate=pl.CostEstimate(
            flops=0, bytes_accessed=4 * slots * math.prod(shape), transcendentals=0
        ),
        name="pack",
    )(index, source)


def tail_kernel(side, picks, batch, *refs):
    pieces = refs[1 : 1 + batch * picks]
    (
        query_ref,
        context_ref,
        image_ref,
        key_ref,
        value_ref,
        out_weight_ref,
        gain_ref,
        up_ref,
        down_ref,
        result_ref,
    ) = refs[1 + batch * picks :]
    area, channels = pieces[0].shape
    head_size = channels // HEADS
    lane = lax.broadcasted_iota(jnp.int32, (area, channels), 1) // head_size
    attended = []
    for region in range(batch):
        rows = pl.ds(region * area, area)
        fetched = jnp.concatenate(
            [piece[...] for piece in pieces[region * picks : (region + 1) * picks]], axis=0
        )
        keys = jnp.dot(fetched, key_ref[...], preferred_element_type=F32).astype(BF16)
        values = jnp.dot(fetched, value_ref[...], preferred_element_type=F32).astype(BF16)
        queries = query_ref[rows, :]
        zero = jnp.zeros_like(queries)
        stacked = jnp.concatenate(
            [jnp.where(lane == head, queries, zero) for head in range(HEADS)], axis=0
        )
        scores = lax.dot_general(
            stacked, keys, (((1,), (1,)), ((), ())), preferred_element_type=F32
        ) * head_size ** (-0.5)
        expons = jnp.exp(scores - jnp.max(scores, axis=-1, keepdims=True))
        weights = (expons * (1.0 / jnp.sum(expons, axis=-1, keepdims=True))).astype(BF16)
        blended = jnp.dot(weights, values, preferred_element_type=F32)
        picked = jnp.zeros((area, channels), F32)
        for head in range(HEADS):
            picked = jnp.where(lane == head, blended[head * area : (head + 1) * area], picked)
        attended.append(picked)
    combined = (jnp.concatenate(attended, axis=0) + context_ref[...]).astype(BF16)
    image = regions_of(image_ref[...].astype(F32), side)
    residual = image + jnp.dot(combined, out_weight_ref[...], preferred_element_type=F32)
    stored = residual.astype(BF16).astype(F32)
    second = normalize(stored, gain_ref[...]).astype(BF16)
    lifted = jnp.dot(second, up_ref[...], preferred_element_type=F32)
    hidden = jax.nn.gelu(lifted, approximate=True).astype(BF16)
    refined = stored + jnp.dot(hidden, down_ref[...], preferred_element_type=F32)
    result_ref[...] = strip_of(refined, side, batch * side).astype(BF16)


def tail(position, table, queries, context, image, weights, side, picks):
    height, width, channels = image.shape
    area = side * side
    per_row = width // side
    batch = math.gcd(per_row, 4)
    halves = per_row // batch

    def piece(which):
        return pl.BlockSpec(
            (None, area, channels),
            lambda i, j, position: (
                position[((i * halves + j) * batch) * picks + which],
                0,
                0,
            ),
        )

    full = lambda a: pl.BlockSpec(a.shape, lambda i, j, position: (0,) * a.ndim)
    tokens = pl.BlockSpec((batch * area, channels), lambda i, j, position: (i * halves + j, 0))
    strip = pl.BlockSpec((side, batch * side, channels), lambda i, j, position: (i, j, 0))
    return pl.pallas_call(
        functools.partial(tail_kernel, side, picks, batch),
        grid_spec=pltpu.PrefetchScalarGridSpec(
            num_scalar_prefetch=1,
            grid=(height // side, halves),
            in_specs=[piece(i) for i in range(batch * picks)]
            + [tokens, tokens, strip]
            + [full(w) for w in weights],
            out_specs=strip,
        ),
        out_shape=jax.ShapeDtypeStruct(image.shape, BF16),
        cost_estimate=pl.CostEstimate(
            flops=image.size * 4000, bytes_accessed=16 * image.size, transcendentals=40 * image.size
        ),
        name="tail",
    )(position, *([table] * (batch * picks)), queries, context, image, *weights)


def body(
    image, routes, norm_gain, qkv_weight, lce_weight, out_weight, mlp_gain, up_weight, down_weight
):
    height, grid_width, channels = image.shape
    col_devices = lax.axis_size("cols")
    devices = lax.axis_size("rows") * col_devices
    region_rows, region_cols, pick_count = routes.shape
    side = height // region_rows
    pair_count = region_rows * region_cols * pick_count
    capacity = max(2, 2 * pair_count // devices)
    all_cols = region_cols * col_devices

    targets = routes.reshape(pair_count)
    target_row = targets // all_cols
    target_col = targets % all_cols
    owners = target_row // region_rows * col_devices + target_col // region_cols
    local_index = target_row % region_rows * region_cols + target_col % region_cols
    pairs = jnp.arange(pair_count, dtype=jnp.int32)
    earlier = (owners[:, None] == owners[None, :]) & (pairs[None, :] < pairs[:, None])
    position = owners * capacity + jnp.sum(earlier.astype(jnp.int32), axis=1)
    slots = jnp.arange(devices * capacity, dtype=jnp.int32)
    requests = jnp.sum(
        jnp.where(position[None, :] == slots[:, None], local_index[None, :], 0), axis=1
    )
    requested = lax.all_to_all(
        requests.reshape(devices, capacity), ("rows", "cols"), 0, 0, tiled=True
    )

    normed = norm_regions(image, norm_gain, side)
    served = pack(normed, requested.reshape(-1), math.gcd(devices, 8))
    table = lax.all_to_all(
        served.reshape(devices, capacity, *normed.shape[1:]), ("rows", "cols"), 0, 0, tiled=True
    ).reshape(served.shape)

    margin = (lce_weight.shape[0] - 1) // 2
    padded = halo(image, (("rows", 0), ("cols", 1)), margin)
    padded = jnp.pad(padded, ((0, 0), (0, -padded.shape[1] % 16), (0, 0)))
    query_value = jnp.concatenate(
        [qkv_weight[:, :channels], qkv_weight[:, 2 * channels :]], axis=1
    )
    context, queries = context_and_queries(
        padded, norm_gain, query_value, lce_weight, side, height, grid_width
    )
    weights = (
        qkv_weight[:, channels : 2 * channels],
        qkv_weight[:, 2 * channels :],
        out_weight,
        mlp_gain.reshape(1, channels),
        up_weight,
        down_weight,
    )
    return tail(position, table, queries, context, image, weights, side, pick_count)


def solution(mesh):
    in_specs = (P("rows", "cols", None), P("rows", "cols", None), P(), P(), P(), P(), P(), P(), P())
    out_specs = P("rows", "cols", None)
    return jax.shard_map(body, mesh=mesh, in_specs=in_specs, out_specs=out_specs, check_vma=False)
```

```python
import functools
import math

import jax
import jax.numpy as jnp
from jax import lax
from jax.experimental import pallas as pl
from jax.experimental.pallas import tpu as pltpu
from jax.sharding import Mesh
from jax.sharding import PartitionSpec as P

HEADS = 4
EPSILON = 1e-06
F32 = jnp.float32
BF16 = jnp.bfloat16


def halo(block, sides, width):
    for axis, dim in sides:
        count = lax.axis_size(axis)
        forward = [(i, i + 1) for i in range(count - 1)]
        backward = [(target, source) for source, target in forward]
        low = lax.ppermute(
            lax.slice_in_dim(block, block.shape[dim] - width, None, axis=dim), axis, forward
        )
        high = lax.ppermute(lax.slice_in_dim(block, 0, width, axis=dim), axis, backward)
        block = jnp.concatenate([low, block, high], axis=dim)
    return block


def normalize(floats, gain):
    centered = floats - jnp.mean(floats, axis=-1, keepdims=True)
    spread = jnp.mean(centered * centered, axis=-1, keepdims=True)
    return centered * lax.rsqrt(spread + EPSILON) * gain


def regions_of(strip, side):
    height, width, channels = strip.shape
    return (
        strip.reshape(height, width // side, side, channels)
        .transpose(1, 0, 2, 3)
        .reshape(height * width, channels)
    )


def strip_of(tokens, side, width):
    channels = tokens.shape[-1]
    return (
        tokens.reshape(width // side, side, side, channels)
        .transpose(1, 0, 2, 3)
        .reshape(side, width, channels)
    )


def norm_kernel(side, image_ref, gain_ref, out_ref):
    normed = normalize(image_ref[...].astype(F32), gain_ref[...])
    out_ref[...] = regions_of(normed, side).astype(BF16).reshape(out_ref.shape)


def norm_regions(image, gain, side):
    height, width, channels = image.shape
    per_row = width // side
    return pl.pallas_call(
        functools.partial(norm_kernel, side),
        grid=(height // side,),
        in_specs=[
            pl.BlockSpec((side, width, channels), lambda i: (i, 0, 0)),
            pl.BlockSpec((1, channels), lambda i: (0, 0)),
        ],
        out_specs=pl.BlockSpec((per_row, side * side, channels), lambda i: (i, 0, 0)),
        out_shape=jax.ShapeDtypeStruct(
            (height // side * per_row, side * side, channels), BF16
        ),
        cost_estimate=pl.CostEstimate(
            flops=10 * image.size, bytes_accessed=4 * image.size, transcendentals=0
        ),
        name="norm_regions",
    )(image, gain.reshape(1, channels))


def context_kernel(side, kernel_size, padded_ref, gain_ref, weight_ref, lce_ref, context_ref, query_ref):
    step = pl.program_id(0)
    rows = side + kernel_size - 1
    channels = padded_ref.shape[-1]
    width = query_ref.shape[0] // side
    strip = padded_ref[pl.ds(step * side, rows)].astype(F32)
    wide = strip.shape[1]
    normed = normalize(strip, gain_ref[...]).astype(BF16).reshape(rows * wide, channels)
    projected = jnp.dot(normed, weight_ref[...], preferred_element_type=F32).astype(BF16)
    values = projected[:, channels:].astype(F32).reshape(rows, wide, channels)
    summed = jnp.zeros((side, width, channels), F32)
    for col in range(kernel_size):
        moved = values if col == 0 else pltpu.roll(values, wide - col, 1)
        moved = moved[:, :width]
        for row in range(kernel_size):
            summed = summed + moved[row : row + side] * lce_ref[row, col]
    context_ref[...] = regions_of(summed, side)
    margin = (kernel_size - 1) // 2
    queries = projected[:, :channels].astype(F32).reshape(rows, wide, channels)
    inner = pltpu.roll(queries, wide - margin, 1)[margin : margin + side, :width]
    query_ref[...] = regions_of(inner, side).astype(BF16)


def context_and_queries(padded, gain, query_value_weight, lce_weight, side, height, width):
    channels = padded.shape[-1]
    kernel_size = lce_weight.shape[0]
    tokens = height * width
    full = lambda shape: pl.BlockSpec(shape, lambda i: (0,) * len(shape))
    return pl.pallas_call(
        functools.partial(context_kernel, side, kernel_size),
        grid=(height // side,),
        in_specs=[
            full(padded.shape),
            full((1, channels)),
            full(query_value_weight.shape),
            full((kernel_size, kernel_size, 1, channels)),
        ],
        out_specs=[
            pl.BlockSpec((side * width, channels), lambda i: (i, 0)),
            pl.BlockSpec((side * width, channels), lambda i: (i, 0)),
        ],
        out_shape=[
            jax.ShapeDtypeStruct((tokens, channels), F32),
            jax.ShapeDtypeStruct((tokens, channels), BF16),
        ],
        cost_estimate=pl.CostEstimate(
            flops=tokens * channels * 600, bytes_accessed=10 * tokens * channels, transcendentals=0
        ),
        name="context",
    )(
        padded,
        gain.reshape(1, channels),
        query_value_weight,
        lce_weight.reshape(kernel_size, kernel_size, 1, channels),
    )


def pack_kernel(chunk, capacity, layers, here_ref, wanted_ref, source_ref, *out_refs):
    for distance, out_ref in enumerate(out_refs, 1):
        base = ((here_ref[0] ^ distance) * layers + (here_ref[1] ^ chunk)) * capacity
        for slot in range(capacity):
            out_ref[slot] = source_ref[wanted_ref[base + slot]]


def pack(source, here, wanted, chunk, peers, layers, capacity):
    shape = (capacity, *source.shape[1:])
    count = peers - 1
    return pl.pallas_call(
        functools.partial(pack_kernel, chunk, capacity, layers),
        grid_spec=pltpu.PrefetchScalarGridSpec(
            num_scalar_prefetch=2,
            grid=(1,),
            in_specs=[pl.BlockSpec(source.shape, lambda i, *_: (0, 0, 0))],
            out_specs=[pl.BlockSpec(shape, lambda i, *_: (0, 0, 0))] * count,
        ),
        out_shape=[jax.ShapeDtypeStruct(shape, source.dtype)] * count,
        cost_estimate=pl.CostEstimate(
            flops=0, bytes_accessed=4 * count * math.prod(shape), transcendentals=0
        ),
        name="pack",
    )(here, wanted, source)


def load_all(sources, landed, sems):
    copies, start = [], 0
    for i, source in enumerate(sources):
        copies.append(
            pltpu.make_async_copy(source, landed.at[pl.ds(start, source.shape[0])], sems.at[i])
        )
        start += source.shape[0]
    for copy in copies:
        copy.start()
    for copy in copies:
        copy.wait()


def collect_kernel(count, position_ref, *refs):
    sources, out_ref, landed, sems = refs[:count], refs[count], refs[-2], refs[-1]
    step = pl.program_id(0)

    @pl.when(step == 0)
    def _():
        load_all(sources, landed, sems)

    total = landed.shape[0]
    per_step = out_ref.shape[0]
    for i in range(per_step):
        at = position_ref[step * per_step + i]
        out_ref[i] = landed[jnp.where(at < total, at, 0)]


def collect(position, sources, steps):
    shape = sources[0].shape[1:]
    total = sum(source.shape[0] for source in sources)
    pairs = position.shape[0]
    return pl.pallas_call(
        functools.partial(collect_kernel, len(sources)),
        grid_spec=pltpu.PrefetchScalarGridSpec(
            num_scalar_prefetch=1,
            grid=(steps,),
            in_specs=[pl.BlockSpec(memory_space=pl.ANY)] * len(sources),
            out_specs=pl.BlockSpec((pairs // steps, *shape), lambda i, _: (i, 0, 0)),
            scratch_shapes=[
                pltpu.VMEM((total, *shape), BF16),
                pltpu.SemaphoreType.DMA((len(sources),)),
            ],
        ),
        out_shape=jax.ShapeDtypeStruct((pairs, *shape), BF16),
        cost_estimate=pl.CostEstimate(
            flops=0, bytes_accessed=2 * (total + pairs) * math.prod(shape), transcendentals=0
        ),
        name="collect",
    )(position, *sources)


def tail_kernel(side, picks, batch, early, late_count, position_ref, *refs):
    late = refs[:late_count]
    (
        fetched_ref,
        query_ref,
        context_ref,
        image_ref,
        key_ref,
        value_ref,
        out_weight_ref,
        gain_ref,
        up_ref,
        down_ref,
        result_ref,
        landed,
        sems,
    ) = refs[late_count:]
    step = pl.program_id(0) * pl.num_programs(1) + pl.program_id(1)

    @pl.when(step == 0)
    def _():
        load_all(late, landed, sems)

    def piece(which):
        at = position_ref[step * (batch * picks) + which]
        is_late = at >= early
        return jnp.where(is_late, landed[jnp.where(is_late, at - early, 0)], fetched_ref[which])

    area, channels = fetched_ref.shape[1:]
    head_size = channels // HEADS
    lane = lax.broadcasted_iota(jnp.int32, (area, channels), 1) // head_size
    attended = []
    for region in range(batch):
        rows = pl.ds(region * area, area)
        fetched = jnp.concatenate(
            [piece(which) for which in range(region * picks, (region + 1) * picks)], axis=0
        )
        keys = jnp.dot(fetched, key_ref[...], preferred_element_type=F32).astype(BF16)
        values = jnp.dot(fetched, value_ref[...], preferred_element_type=F32).astype(BF16)
        queries = query_ref[rows, :]
        zero = jnp.zeros_like(queries)
        stacked = jnp.concatenate(
            [jnp.where(lane == head, queries, zero) for head in range(HEADS)], axis=0
        )
        scores = lax.dot_general(
            stacked, keys, (((1,), (1,)), ((), ())), preferred_element_type=F32
        ) * head_size ** (-0.5)
        expons = jnp.exp(scores - jnp.max(scores, axis=-1, keepdims=True))
        weights = (expons * (1.0 / jnp.sum(expons, axis=-1, keepdims=True))).astype(BF16)
        blended = jnp.dot(weights, values, preferred_element_type=F32)
        picked = jnp.zeros((area, channels), F32)
        for head in range(HEADS):
            picked = jnp.where(lane == head, blended[head * area : (head + 1) * area], picked)
        attended.append(picked)
    combined = (jnp.concatenate(attended, axis=0) + context_ref[...]).astype(BF16)
    image = regions_of(image_ref[...].astype(F32), side)
    residual = image + jnp.dot(combined, out_weight_ref[...], preferred_element_type=F32)
    stored = residual.astype(BF16).astype(F32)
    second = normalize(stored, gain_ref[...]).astype(BF16)
    lifted = jnp.dot(second, up_ref[...], preferred_element_type=F32)
    hidden = jax.nn.gelu(lifted, approximate=True).astype(BF16)
    refined = stored + jnp.dot(hidden, down_ref[...], preferred_element_type=F32)
    result_ref[...] = strip_of(refined, side, batch * side).astype(BF16)


def tail(position, early, fetched, late, queries, context, image, weights, side, picks):
    height, width, channels = image.shape
    area = side * side
    per_row = width // side
    batch = math.gcd(per_row, 4)
    halves = per_row // batch
    full = lambda a: pl.BlockSpec(a.shape, lambda i, j, position: (0,) * a.ndim)
    tokens = pl.BlockSpec((batch * area, channels), lambda i, j, position: (i * halves + j, 0))
    strip = pl.BlockSpec((side, batch * side, channels), lambda i, j, position: (i, j, 0))
    regions = pl.BlockSpec(
        (batch * picks, area, channels), lambda i, j, position: (i * halves + j, 0, 0)
    )
    total = sum(a.shape[0] for a in late)
    return pl.pallas_call(
        functools.partial(tail_kernel, side, picks, batch, early, len(late)),
        grid_spec=pltpu.PrefetchScalarGridSpec(
            num_scalar_prefetch=1,
            grid=(height // side, halves),
            in_specs=[pl.BlockSpec(memory_space=pl.ANY)] * len(late)
            + [regions, tokens, tokens, strip]
            + [full(w) for w in weights],
            out_specs=strip,
            scratch_shapes=[
                pltpu.VMEM((total, area, channels), BF16),
                pltpu.SemaphoreType.DMA((len(late),)),
            ],
        ),
        out_shape=jax.ShapeDtypeStruct(image.shape, BF16),
        cost_estimate=pl.CostEstimate(
            flops=image.size * 4000, bytes_accessed=16 * image.size, transcendentals=40 * image.size
        ),
        name="tail",
    )(position, *late, fetched, queries, context, image, *weights)


def body(
    image, routes, norm_gain, qkv_weight, lce_weight, out_weight, mlp_gain, up_weight, down_weight
):
    height, grid_width, channels = image.shape
    layers, across = lax.axis_size("z"), lax.axis_size("x")
    peers = lax.axis_size("rows") * across
    devices = peers * layers
    region_rows, region_cols, pick_count = routes.shape
    side = height // region_rows
    pair_count = region_rows * region_cols * pick_count
    capacity = max(2, 2 * pair_count // devices)
    all_cols = region_cols * layers * across

    regions = region_rows * region_cols
    peer = lax.axis_index("rows") * across + lax.axis_index("x")
    layer = lax.axis_index("z")
    here = jnp.stack([peer, layer])

    targets = routes.reshape(pair_count)
    target_row = targets // all_cols
    target_col = targets % all_cols
    owner_col = target_col // region_cols
    owner_layer = owner_col // across
    owner_peer = target_row // region_rows * across + owner_col % across
    local_index = target_row % region_rows * region_cols + target_col % region_cols
    owners = owner_peer * layers + owner_layer
    pairs = jnp.arange(pair_count, dtype=jnp.int32)
    earlier = (owners[:, None] == owners[None, :]) & (pairs[None, :] < pairs[:, None])
    slot = jnp.sum(earlier.astype(jnp.int32), axis=1)
    distance = owner_peer ^ peer
    per_layer = regions + (peers - 1) * capacity
    position = (owner_layer ^ layer) * per_layer + jnp.where(
        distance == 0, local_index, regions + (distance - 1) * capacity + slot
    )
    asked = owners * capacity + slot
    slots = jnp.arange(devices * capacity, dtype=jnp.int32)
    requests = jnp.sum(
        jnp.where(asked[None, :] == slots[:, None], local_index[None, :], 0), axis=1
    )
    wanted = lax.all_to_all(
        requests.reshape(peers, layers * capacity), ("rows", "x"), 0, 0, tiled=True
    ).reshape(-1)

    normed = norm_regions(image, norm_gain, side)

    def from_layer(block, step):
        return lax.ppermute(block, "z", [(i, i ^ step) for i in range(layers)])

    arrived = []
    early = 0
    held = [normed]
    for step in range(1, layers):
        block = normed
        if step > 2:
            block, _ = lax.optimization_barrier((normed, held[step - 2]))
        held.append(from_layer(block, step))
    for step, source in enumerate(held):
        packed = pack(source, here, wanted, step, peers, layers, capacity)
        got = [
            lax.ppermute(part, ("rows", "x"), [(i, i ^ far) for i in range(peers)])
            for far, part in enumerate(packed, 1)
        ]
        arrived.append([source, *got])
    late = arrived.pop()
    early = per_layer * len(arrived)
    fetched = collect(position, sum(arrived, []), math.gcd(pair_count, 8))

    margin = (lce_weight.shape[0] - 1) // 2
    padded = halo(image, (("rows", 0), (("z", "x"), 1)), margin)
    padded = jnp.pad(padded, ((0, 0), (0, -padded.shape[1] % 16), (0, 0)))
    query_value = jnp.concatenate(
        [qkv_weight[:, :channels], qkv_weight[:, 2 * channels :]], axis=1
    )
    context, queries = context_and_queries(
        padded, norm_gain, query_value, lce_weight, side, height, grid_width
    )
    weights = (
        qkv_weight[:, channels : 2 * channels],
        qkv_weight[:, 2 * channels :],
        out_weight,
        mlp_gain.reshape(1, channels),
        up_weight,
        down_weight,
    )
    return tail(position, early, fetched, late, queries, context, image, weights, side, pick_count)


def solution(mesh):
    devices = mesh.devices
    layers = len({device.coords[2] for device in devices[0]})
    split = Mesh(
        devices.reshape(devices.shape[0], layers, devices.shape[1] // layers), ("rows", "z", "x")
    )
    grid = P("rows", ("z", "x"), None)
    in_specs = (grid, grid, P(), P(), P(), P(), P(), P(), P())
    return jax.shard_map(body, mesh=split, in_specs=in_specs, out_specs=grid, check_vma=False)
```

```python
import functools
import math

import jax
import jax.numpy as jnp
from jax import lax
from jax.experimental import pallas as pl
from jax.experimental.pallas import tpu as pltpu
from jax.sharding import Mesh
from jax.sharding import PartitionSpec as P

HEADS = 4
PAIR = 2
EPSILON = 1e-06
F32 = jnp.float32
BF16 = jnp.bfloat16


def halo(block, sides, width):
    for axis, dim in sides:
        count = lax.axis_size(axis)
        forward = [(i, i + 1) for i in range(count - 1)]
        backward = [(target, source) for source, target in forward]
        low = lax.ppermute(
            lax.slice_in_dim(block, block.shape[dim] - width, None, axis=dim), axis, forward
        )
        high = lax.ppermute(lax.slice_in_dim(block, 0, width, axis=dim), axis, backward)
        block = jnp.concatenate([low, block, high], axis=dim)
    return block


def normalize(floats, gain):
    centered = floats - jnp.mean(floats, axis=-1, keepdims=True)
    spread = jnp.mean(centered * centered, axis=-1, keepdims=True)
    return centered * lax.rsqrt(spread + EPSILON) * gain


def regions_of(strip, side):
    height, width, channels = strip.shape
    return (
        strip.reshape(height, width // side, side, channels)
        .transpose(1, 0, 2, 3)
        .reshape(height * width, channels)
    )


def strip_of(tokens, side, width):
    channels = tokens.shape[-1]
    return (
        tokens.reshape(width // side, side, side, channels)
        .transpose(1, 0, 2, 3)
        .reshape(side, width, channels)
    )


def norm_kernel(side, image_ref, gain_ref, out_ref):
    normed = normalize(image_ref[...].astype(F32), gain_ref[...])
    out_ref[...] = regions_of(normed, side).astype(BF16).reshape(out_ref.shape)


def norm_regions(image, gain, side):
    height, width, channels = image.shape
    per_row = width // side
    return pl.pallas_call(
        functools.partial(norm_kernel, side),
        grid=(height // side,),
        in_specs=[
            pl.BlockSpec((side, width, channels), lambda i: (i, 0, 0)),
            pl.BlockSpec((1, channels), lambda i: (0, 0)),
        ],
        out_specs=pl.BlockSpec((per_row, side * side, channels), lambda i: (i, 0, 0)),
        out_shape=jax.ShapeDtypeStruct(
            (height // side * per_row, side * side, channels), BF16
        ),
        cost_estimate=pl.CostEstimate(
            flops=10 * image.size, bytes_accessed=4 * image.size, transcendentals=0
        ),
        name="norm_regions",
    )(image, gain.reshape(1, channels))


def context_kernel(side, kernel_size, padded_ref, gain_ref, weight_ref, lce_ref, context_ref, query_ref):
    step = pl.program_id(0)
    rows = side + kernel_size - 1
    channels = padded_ref.shape[-1]
    width = query_ref.shape[0] // side
    strip = padded_ref[pl.ds(step * side, rows)].astype(F32)
    wide = strip.shape[1]
    normed = normalize(strip, gain_ref[...]).astype(BF16).reshape(rows * wide, channels)
    weight = jnp.concatenate([weight_ref[:, :channels], weight_ref[:, 2 * channels :]], axis=1)
    projected = jnp.dot(normed, weight, preferred_element_type=F32).astype(BF16)
    values = projected[:, channels:].astype(F32).reshape(rows, wide, channels)
    summed = jnp.zeros((side, width, channels), F32)
    for col in range(kernel_size):
        moved = values if col == 0 else pltpu.roll(values, wide - col, 1)
        moved = moved[:, :width]
        for row in range(kernel_size):
            summed = summed + moved[row : row + side] * lce_ref[row, pl.ds(col, 1), :]
    context_ref[...] = regions_of(summed, side)
    margin = (kernel_size - 1) // 2
    queries = projected[:, :channels].astype(F32).reshape(rows, wide, channels)
    inner = pltpu.roll(queries, wide - margin, 1)[margin : margin + side, :width]
    query_ref[...] = regions_of(inner, side).astype(BF16)


def context_and_queries(padded, gain, qkv_weight, lce_weight, side, height, width):
    channels = padded.shape[-1]
    kernel_size = lce_weight.shape[0]
    tokens = height * width
    full = lambda shape: pl.BlockSpec(shape, lambda i: (0,) * len(shape))
    return pl.pallas_call(
        functools.partial(context_kernel, side, kernel_size),
        grid=(height // side,),
        in_specs=[
            full(padded.shape),
            full((1, channels)),
            full(qkv_weight.shape),
            full(lce_weight.shape),
        ],
        out_specs=[
            pl.BlockSpec((side * width, channels), lambda i: (i, 0)),
            pl.BlockSpec((side * width, channels), lambda i: (i, 0)),
        ],
        out_shape=[
            jax.ShapeDtypeStruct((tokens, channels), F32),
            jax.ShapeDtypeStruct((tokens, channels), BF16),
        ],
        cost_estimate=pl.CostEstimate(
            flops=tokens * channels * 600, bytes_accessed=10 * tokens * channels, transcendentals=0
        ),
        name="context",
    )(
        padded,
        gain.reshape(1, channels),
        qkv_weight,
        lce_weight,
    )


def pack_kernel(chunk, capacity, layers, here_ref, wanted_ref, source_ref, *out_refs):
    for distance, out_ref in enumerate(out_refs, 1):
        base = ((here_ref[0] ^ distance) * layers + (here_ref[1] ^ chunk)) * capacity
        for slot in range(capacity):
            out_ref[slot] = source_ref[wanted_ref[base + slot]]


def pack(source, here, wanted, chunk, peers, layers, capacity):
    shape = (capacity, *source.shape[1:])
    count = peers - 1
    return pl.pallas_call(
        functools.partial(pack_kernel, chunk, capacity, layers),
        grid_spec=pltpu.PrefetchScalarGridSpec(
            num_scalar_prefetch=2,
            grid=(1,),
            in_specs=[pl.BlockSpec(source.shape, lambda i, *_: (0, 0, 0))],
            out_specs=[pl.BlockSpec(shape, lambda i, *_: (0, 0, 0))] * count,
        ),
        out_shape=[jax.ShapeDtypeStruct(shape, source.dtype)] * count,
        cost_estimate=pl.CostEstimate(
            flops=0, bytes_accessed=4 * count * math.prod(shape), transcendentals=0
        ),
        name="pack",
    )(here, wanted, source)


def load_all(sources, landed, sems):
    copies, start = [], 0
    for i, source in enumerate(sources):
        copies.append(
            pltpu.make_async_copy(source, landed.at[pl.ds(start, source.shape[0])], sems.at[i])
        )
        start += source.shape[0]
    for copy in copies:
        copy.start()
    for copy in copies:
        copy.wait()


def collect_kernel(count, position_ref, *refs):
    sources, out_ref, landed, sems = refs[:count], refs[count], refs[-2], refs[-1]
    step = pl.program_id(0)

    @pl.when(step == 0)
    def _():
        load_all(sources, landed, sems)

    total = landed.shape[0]
    per_step = out_ref.shape[0]
    for i in range(per_step):
        at = position_ref[step * per_step + i]
        out_ref[i] = landed[jnp.where(at < total, at, 0)]


def collect(position, sources, steps):
    shape = sources[0].shape[1:]
    total = sum(source.shape[0] for source in sources)
    pairs = position.shape[0]
    return pl.pallas_call(
        functools.partial(collect_kernel, len(sources)),
        grid_spec=pltpu.PrefetchScalarGridSpec(
            num_scalar_prefetch=1,
            grid=(steps,),
            in_specs=[pl.BlockSpec(memory_space=pl.ANY)] * len(sources),
            out_specs=pl.BlockSpec((pairs // steps, *shape), lambda i, _: (i, 0, 0)),
            scratch_shapes=[
                pltpu.VMEM((total, *shape), BF16),
                pltpu.SemaphoreType.DMA((len(sources),)),
            ],
        ),
        out_shape=jax.ShapeDtypeStruct((pairs, *shape), BF16),
        cost_estimate=pl.CostEstimate(
            flops=0, bytes_accessed=2 * (total + pairs) * math.prod(shape), transcendentals=0
        ),
        name="collect",
    )(position, *sources)


def project(fetched, weight_ref):
    channels = fetched.shape[-1]
    projected = jnp.dot(
        fetched, weight_ref[:, channels : 3 * channels], preferred_element_type=F32
    ).astype(BF16)
    keys, values = projected[:, :channels], projected[:, channels:]
    return keys, jnp.concatenate([values, jnp.ones_like(values)], axis=1)


def score(queries, keys):
    area, channels = queries.shape
    lane = lax.broadcasted_iota(jnp.int32, (area, channels), 1) // (channels // HEADS)
    zero = jnp.zeros_like(queries)
    stacked = jnp.concatenate(
        [jnp.where(lane == head, queries, zero) for head in range(HEADS)], axis=0
    )
    return lax.dot_general(
        stacked, keys, (((1,), (1,)), ((), ())), preferred_element_type=F32
    )


def weigh(scores, exponent):
    highest = jnp.max(scores, axis=-1, keepdims=True)
    return jnp.exp2((scores - highest) * exponent).astype(BF16)


def blend(weights, extended):
    area, channels = weights.shape[0] // HEADS, extended.shape[1] // 2
    blended = jnp.dot(weights, extended, preferred_element_type=F32)
    lane = lax.broadcasted_iota(jnp.int32, (area, channels), 1) // (channels // HEADS)
    top, low = blended[:area, :channels], blended[:area, channels:]
    for head in range(1, HEADS):
        rows = slice(head * area, (head + 1) * area)
        top = jnp.where(lane == head, blended[rows, :channels], top)
        low = jnp.where(lane == head, blended[rows, channels:], low)
    return top * (1.0 / low)


def gelu(lifted):
    inner = lifted * (0.7978845608028654 + 0.035677408136300125 * (lifted * lifted))
    return lifted * (0.5 + 0.5 * jnp.tanh(inner))


def tail_kernel(side, picks, batch, early, late_count, position_ref, *refs):
    late = refs[:late_count]
    (
        fetched_ref,
        query_ref,
        context_ref,
        image_ref,
        qkv_ref,
        out_weight_ref,
        gain_ref,
        up_ref,
        down_ref,
        result_ref,
        landed,
        combined_ref,
        sems,
    ) = refs[late_count:]
    step = pl.program_id(0)
    last = pl.num_programs(0) - 2

    @pl.when(step == 0)
    def _():
        combined_ref[...] = jnp.zeros_like(combined_ref)
        load_all(late, landed, sems)

    area, channels = fetched_ref.shape[1:]
    exponent = (channels // HEADS) ** (-0.5) * math.log2(math.e)
    first = jnp.minimum(step, last) * (batch * picks)

    def piece(which):
        at = position_ref[first + which]
        is_late = at >= early
        return jnp.where(is_late, landed[jnp.where(is_late, at - early, 0)], fetched_ref[which])

    previous = combined_ref[...]
    chunk = PAIR * area

    def attention(region):
        rows = pl.ds(region * area, area)
        fetched = jnp.concatenate(
            [piece(which) for which in range(region * picks, (region + 1) * picks)], axis=0
        )
        keys, extended = project(fetched, qkv_ref)
        yield True
        scores = score(query_ref[rows, :], keys)
        yield True
        weights = weigh(scores, exponent)
        yield True
        attended = blend(weights, extended)
        combined_ref[rows, :] = (attended + context_ref[rows, :]).astype(BF16)
        yield True

    def feed_forward(part):
        columns = pl.ds(part * PAIR * side, PAIR * side)
        image = regions_of(image_ref[:, columns, :].astype(F32), side)
        combined = previous[part * chunk : (part + 1) * chunk]
        residual = image + jnp.dot(combined, out_weight_ref[...], preferred_element_type=F32)
        yield True
        stored = residual.astype(BF16).astype(F32)
        second = normalize(stored, gain_ref[...]).astype(BF16)
        yield True
        lifted = jnp.dot(second, up_ref[...], preferred_element_type=F32)
        yield True
        hidden = gelu(lifted).astype(BF16)
        yield True
        refined = stored + jnp.dot(hidden, down_ref[...], preferred_element_type=F32)
        result_ref[:, columns, :] = strip_of(refined, side, PAIR * side).astype(BF16)
        yield True

    lines = [feed_forward(part) for part in range(batch // PAIR)]
    lines += [attention(region) for region in range(batch)]
    while lines:
        lines = [line for line in lines if next(line, None) is not None]


def tail(position, early, fetched, late, queries, context, image, weights, side, picks):
    height, width, channels = image.shape
    area = side * side
    per_row = width // side
    batch = math.gcd(per_row, 4)
    halves = per_row // batch
    steps = height // side * halves
    full = lambda a: pl.BlockSpec(a.shape, lambda i, position: (0,) * a.ndim)
    now = lambda i: jnp.minimum(i, steps - 1)
    before = lambda i: jnp.maximum(i - 1, 0)
    tokens = pl.BlockSpec((batch * area, channels), lambda i, position: (now(i), 0))
    strip = pl.BlockSpec(
        (side, batch * side, channels),
        lambda i, position: (before(i) // halves, before(i) % halves, 0),
    )
    regions = pl.BlockSpec((batch * picks, area, channels), lambda i, position: (now(i), 0, 0))
    total = sum(a.shape[0] for a in late)
    return pl.pallas_call(
        functools.partial(tail_kernel, side, picks, batch, early, len(late)),
        grid_spec=pltpu.PrefetchScalarGridSpec(
            num_scalar_prefetch=1,
            grid=(steps + 1,),
            in_specs=[pl.BlockSpec(memory_space=pl.ANY)] * len(late)
            + [regions, tokens, tokens, strip]
            + [full(w) for w in weights],
            out_specs=strip,
            scratch_shapes=[
                pltpu.VMEM((total, area, channels), BF16),
                pltpu.VMEM((batch * area, channels), BF16),
                pltpu.SemaphoreType.DMA((len(late),)),
            ],
        ),
        out_shape=jax.ShapeDtypeStruct(image.shape, BF16),
        cost_estimate=pl.CostEstimate(
            flops=image.size * 4000, bytes_accessed=16 * image.size, transcendentals=40 * image.size
        ),
        name="tail",
    )(position, *late, fetched, queries, context, image, *weights)


def body(
    image, routes, norm_gain, qkv_weight, lce_weight, out_weight, mlp_gain, up_weight, down_weight
):
    height, grid_width, channels = image.shape
    layers, across = lax.axis_size("z"), lax.axis_size("x")
    peers = lax.axis_size("rows") * across
    devices = peers * layers
    region_rows, region_cols, pick_count = routes.shape
    side = height // region_rows
    pair_count = region_rows * region_cols * pick_count
    capacity = max(2, 2 * pair_count // devices)
    all_cols = region_cols * layers * across

    regions = region_rows * region_cols
    peer = lax.axis_index("rows") * across + lax.axis_index("x")
    layer = lax.axis_index("z")
    here = jnp.stack([peer, layer])

    targets = routes.reshape(pair_count)
    target_row = targets // all_cols
    target_col = targets % all_cols
    owner_col = target_col // region_cols
    owner_layer = owner_col // across
    owner_peer = target_row // region_rows * across + owner_col % across
    local_index = target_row % region_rows * region_cols + target_col % region_cols
    owners = owner_peer * layers + owner_layer
    pairs = jnp.arange(pair_count, dtype=jnp.int32)
    earlier = (owners[:, None] == owners[None, :]) & (pairs[None, :] < pairs[:, None])
    slot = jnp.sum(earlier.astype(jnp.int32), axis=1)
    distance = owner_peer ^ peer
    per_layer = regions + (peers - 1) * capacity
    position = (owner_layer ^ layer) * per_layer + jnp.where(
        distance == 0, local_index, regions + (distance - 1) * capacity + slot
    )
    asked = owners * capacity + slot
    slots = jnp.arange(devices * capacity, dtype=jnp.int32)
    requests = jnp.sum(
        jnp.where(asked[None, :] == slots[:, None], local_index[None, :], 0), axis=1
    )
    wanted = lax.all_to_all(
        requests.reshape(peers, layers * capacity), ("rows", "x"), 0, 0, tiled=True
    ).reshape(-1)

    normed = norm_regions(image, norm_gain, side)

    def from_layer(block, step):
        return lax.ppermute(block, "z", [(i, i ^ step) for i in range(layers)])

    arrived = []
    early = 0
    held = [normed]
    for step in range(1, layers):
        block = normed
        if step > 2:
            block, _ = lax.optimization_barrier((normed, held[step - 2]))
        held.append(from_layer(block, step))
    for step, source in enumerate(held):
        packed = pack(source, here, wanted, step, peers, layers, capacity)
        got = [
            lax.ppermute(part, ("rows", "x"), [(i, i ^ far) for i in range(peers)])
            for far, part in enumerate(packed, 1)
        ]
        arrived.append([source, *got])
    late = arrived.pop()
    early = per_layer * len(arrived)
    fetched = collect(position, sum(arrived, []), math.gcd(pair_count, 8))

    margin = (lce_weight.shape[0] - 1) // 2
    padded = halo(image, (("rows", 0), (("z", "x"), 1)), margin)
    padded = jnp.pad(padded, ((0, 0), (0, -padded.shape[1] % 16), (0, 0)))
    context, queries = context_and_queries(
        padded, norm_gain, qkv_weight, lce_weight, side, height, grid_width
    )
    weights = (
        qkv_weight,
        out_weight,
        mlp_gain.reshape(1, channels),
        up_weight,
        down_weight,
    )
    return tail(position, early, fetched, late, queries, context, image, weights, side, pick_count)


def solution(mesh):
    devices = mesh.devices
    layers = len({device.coords[2] for device in devices[0]})
    split = Mesh(
        devices.reshape(devices.shape[0], layers, devices.shape[1] // layers), ("rows", "z", "x")
    )
    grid = P("rows", ("z", "x"), None)
    in_specs = (grid, grid, P(), P(), P(), P(), P(), P(), P())
    return jax.shard_map(body, mesh=split, in_specs=in_specs, out_specs=grid, check_vma=False)
```

```python
import functools
import math

import jax
import jax.numpy as jnp
from jax import lax
from jax.experimental import pallas as pl
from jax.experimental.pallas import tpu as pltpu
from jax.sharding import Mesh
from jax.sharding import PartitionSpec as P

HEADS = 4
PAIR = 2
EPSILON = 1e-06
F32 = jnp.float32
BF16 = jnp.bfloat16


def from_sides(low, high, axis):
    count = math.prod(lax.axis_size(name) for name in (axis if isinstance(axis, tuple) else (axis,)))
    forward = [(i, i + 1) for i in range(count - 1)]
    backward = [(target, source) for source, target in forward]
    return lax.ppermute(high, axis, forward), lax.ppermute(low, axis, backward)


def halo(image, margin, border):
    above, below = from_sides(image[:margin], image[-margin:], "rows")
    edges = lambda columns: jnp.concatenate(
        [above[:, columns], image[:, columns], below[:, columns]], axis=0
    )
    left, right = from_sides(
        edges(slice(0, border)), edges(slice(image.shape[1] - border, None)), ("z", "x")
    )
    return above, below, left, right


def normalize(floats, gain):
    centered = floats - jnp.mean(floats, axis=-1, keepdims=True)
    spread = jnp.mean(centered * centered, axis=-1, keepdims=True)
    return centered * lax.rsqrt(spread + EPSILON) * gain


def regions_of(strip, side):
    height, width, channels = strip.shape
    return (
        strip.reshape(height, width // side, side, channels)
        .transpose(1, 0, 2, 3)
        .reshape(height * width, channels)
    )


def strip_of(tokens, side, width):
    channels = tokens.shape[-1]
    return (
        tokens.reshape(width // side, side, side, channels)
        .transpose(1, 0, 2, 3)
        .reshape(side, width, channels)
    )


def norm_kernel(side, image_ref, gain_ref, out_ref):
    normed = normalize(image_ref[...].astype(F32), gain_ref[...])
    out_ref[...] = regions_of(normed, side).astype(BF16).reshape(out_ref.shape)


def norm_regions(image, gain, side):
    height, width, channels = image.shape
    per_row = width // side
    return pl.pallas_call(
        functools.partial(norm_kernel, side),
        grid=(height // side,),
        in_specs=[
            pl.BlockSpec((side, width, channels), lambda i: (i, 0, 0)),
            pl.BlockSpec((1, channels), lambda i: (0, 0)),
        ],
        out_specs=pl.BlockSpec((per_row, side * side, channels), lambda i: (i, 0, 0)),
        out_shape=jax.ShapeDtypeStruct(
            (height // side * per_row, side * side, channels), BF16
        ),
        cost_estimate=pl.CostEstimate(
            flops=10 * image.size, bytes_accessed=4 * image.size, transcendentals=0
        ),
        name="norm_regions",
    )(image, gain.reshape(1, channels))


def context_kernel(
    side,
    margin,
    image_ref,
    above_ref,
    below_ref,
    left_ref,
    right_ref,
    gain_ref,
    weight_ref,
    lce_ref,
    context_ref,
    query_ref,
    padded,
):
    step = pl.program_id(0)
    height, width, channels = image_ref.shape
    border = left_ref.shape[1]

    @pl.when(step == 0)
    def _():
        inner = pl.ds(border, width)
        padded[:margin, inner] = above_ref[...].astype(F32)
        padded[pl.ds(margin, height), inner] = image_ref[...].astype(F32)
        padded[pl.ds(margin + height, margin), inner] = below_ref[...].astype(F32)
        padded[:, :border] = left_ref[...].astype(F32)
        padded[:, pl.ds(border + width, border)] = right_ref[...].astype(F32)

    rows = side + 2 * margin
    strip = padded[pl.ds(step * side, rows)]
    wide = strip.shape[1]
    normed = normalize(strip, gain_ref[...]).astype(BF16).reshape(rows * wide, channels)
    weight = jnp.concatenate([weight_ref[:, :channels], weight_ref[:, 2 * channels :]], axis=1)
    projected = jnp.dot(normed, weight, preferred_element_type=F32).astype(BF16)
    values = projected[:, channels:].astype(F32).reshape(rows, wide, channels)
    summed = jnp.zeros((side, width, channels), F32)
    for col in range(2 * margin + 1):
        moved = pltpu.roll(values, wide - (border - margin + col), 1)[:, :width]
        for row in range(2 * margin + 1):
            summed = summed + moved[row : row + side] * lce_ref[row, pl.ds(col, 1), :]
    context_ref[...] = regions_of(summed, side)
    queries = projected[:, :channels].astype(F32).reshape(rows, wide, channels)
    inner = queries[margin : margin + side, border : border + width]
    query_ref[...] = regions_of(inner, side).astype(BF16)


def context_and_queries(image, around, gain, qkv_weight, lce_weight, side, margin):
    height, width, channels = image.shape
    border = around[-1].shape[1]
    tokens = height * width
    full = lambda a: pl.BlockSpec(a.shape, lambda i: (0,) * a.ndim)
    operands = (image, *around, gain.reshape(1, channels), qkv_weight, lce_weight)
    return pl.pallas_call(
        functools.partial(context_kernel, side, margin),
        grid=(height // side,),
        in_specs=[full(a) for a in operands],
        out_specs=[
            pl.BlockSpec((side * width, channels), lambda i: (i, 0)),
            pl.BlockSpec((side * width, channels), lambda i: (i, 0)),
        ],
        out_shape=[
            jax.ShapeDtypeStruct((tokens, channels), F32),
            jax.ShapeDtypeStruct((tokens, channels), BF16),
        ],
        scratch_shapes=[
            pltpu.VMEM((height + 2 * margin, width + 2 * border, channels), F32),
        ],
        cost_estimate=pl.CostEstimate(
            flops=tokens * channels * 600, bytes_accessed=10 * tokens * channels, transcendentals=0
        ),
        name="context",
    )(*operands)


def pack_kernel(chunks, capacity, layers, here_ref, wanted_ref, *refs):
    sources, out_refs = refs[: len(chunks)], refs[len(chunks) :]
    for distance, out_ref in enumerate(out_refs, 1):
        for place, (chunk, source_ref) in enumerate(zip(chunks, sources)):
            base = ((here_ref[0] ^ distance) * layers + (here_ref[1] ^ chunk)) * capacity
            for slot in range(capacity):
                out_ref[place * capacity + slot] = source_ref[wanted_ref[base + slot]]


def pack(sources, here, wanted, chunks, peers, layers, capacity):
    tile = sources[0].shape
    shape = (capacity * len(chunks), *tile[1:])
    count = peers - 1
    return pl.pallas_call(
        functools.partial(pack_kernel, chunks, capacity, layers),
        grid_spec=pltpu.PrefetchScalarGridSpec(
            num_scalar_prefetch=2,
            grid=(1,),
            in_specs=[pl.BlockSpec(tile, lambda i, *_: (0, 0, 0))] * len(chunks),
            out_specs=[pl.BlockSpec(shape, lambda i, *_: (0, 0, 0))] * count,
        ),
        out_shape=[jax.ShapeDtypeStruct(shape, BF16)] * count,
        cost_estimate=pl.CostEstimate(
            flops=0, bytes_accessed=4 * count * math.prod(shape), transcendentals=0
        ),
        name="pack",
    )(here, wanted, *sources)


def load_all(sources, landed, sems):
    copies, start = [], 0
    for i, source in enumerate(sources):
        copies.append(
            pltpu.make_async_copy(source, landed.at[pl.ds(start, source.shape[0])], sems.at[i])
        )
        start += source.shape[0]
    for copy in copies:
        copy.start()
    for copy in copies:
        copy.wait()


def collect_kernel(count, position_ref, *refs):
    sources, out_ref, landed, sems = refs[:count], refs[count], refs[-2], refs[-1]
    step = pl.program_id(0)

    @pl.when(step == 0)
    def _():
        load_all(sources, landed, sems)

    total = landed.shape[0]
    per_step = out_ref.shape[0]
    for i in range(per_step):
        at = position_ref[step * per_step + i]
        out_ref[i] = landed[jnp.where(at < total, at, 0)]


def collect(position, sources, steps):
    shape = sources[0].shape[1:]
    total = sum(source.shape[0] for source in sources)
    pairs = position.shape[0]
    return pl.pallas_call(
        functools.partial(collect_kernel, len(sources)),
        grid_spec=pltpu.PrefetchScalarGridSpec(
            num_scalar_prefetch=1,
            grid=(steps,),
            in_specs=[pl.BlockSpec(memory_space=pl.ANY)] * len(sources),
            out_specs=pl.BlockSpec((pairs // steps, *shape), lambda i, _: (i, 0, 0)),
            scratch_shapes=[
                pltpu.VMEM((total, *shape), BF16),
                pltpu.SemaphoreType.DMA((len(sources),)),
            ],
        ),
        out_shape=jax.ShapeDtypeStruct((pairs, *shape), BF16),
        cost_estimate=pl.CostEstimate(
            flops=0, bytes_accessed=2 * (total + pairs) * math.prod(shape), transcendentals=0
        ),
        name="collect",
    )(position, *sources)


def project(fetched, weight_ref):
    channels = fetched.shape[-1]
    projected = jnp.dot(
        fetched, weight_ref[:, channels : 3 * channels], preferred_element_type=F32
    ).astype(BF16)
    return projected[:, :channels], projected[:, channels:]


def score(queries, keys):
    area, channels = queries.shape
    lane = lax.broadcasted_iota(jnp.int32, (area, channels), 1) // (channels // HEADS)
    zero = jnp.zeros_like(queries)
    stacked = jnp.concatenate(
        [jnp.where(lane == head, queries, zero) for head in range(HEADS)], axis=0
    )
    return lax.dot_general(
        stacked, keys, (((1,), (1,)), ((), ())), preferred_element_type=F32
    )


def blend(weights, values):
    area, channels = weights.shape[0] // HEADS, values.shape[1]
    blended = jnp.dot(weights, values, preferred_element_type=F32)
    lane = lax.broadcasted_iota(jnp.int32, (area, channels), 1) // (channels // HEADS)
    picked = blended[:area]
    for head in range(1, HEADS):
        picked = jnp.where(lane == head, blended[head * area : (head + 1) * area], picked)
    return picked


def gelu(lifted):
    inner = lifted * (0.7978845608028654 + 0.035677408136300125 * (lifted * lifted))
    return lifted * (0.5 + 0.5 * jnp.tanh(inner))


def tail_kernel(side, picks, batch, early, late_count, position_ref, *refs):
    late = refs[:late_count]
    (
        fetched_ref,
        query_ref,
        context_ref,
        image_ref,
        qkv_ref,
        out_weight_ref,
        gain_ref,
        up_ref,
        down_ref,
        result_ref,
        landed,
        combined_ref,
        sems,
    ) = refs[late_count:]
    step = pl.program_id(0)
    last = pl.num_programs(0) - 2

    @pl.when(step == 0)
    def _():
        combined_ref[...] = jnp.zeros_like(combined_ref)
        load_all(late, landed, sems)

    area, channels = fetched_ref.shape[1:]
    exponent = (channels // HEADS) ** (-0.5) * math.log2(math.e)
    first = jnp.minimum(step, last) * (batch * picks)

    def piece(which):
        at = position_ref[first + which]
        is_late = at >= early
        return jnp.where(is_late, landed[jnp.where(is_late, at - early, 0)], fetched_ref[which])

    previous = combined_ref[...]
    chunk = PAIR * area

    def attention(region):
        rows = pl.ds(region * area, area)
        fetched = jnp.concatenate(
            [piece(which) for which in range(region * picks, (region + 1) * picks)], axis=0
        )
        keys, values = project(fetched, qkv_ref)
        yield True
        scores = score(query_ref[rows, :], keys)
        yield True
        highest = jnp.max(scores, axis=-1, keepdims=True)
        expons = jnp.exp2((scores - highest) * exponent)
        yield True
        total = jnp.sum(expons, axis=-1, keepdims=True)
        weights = (expons * (1.0 / total)).astype(BF16)
        yield True
        attended = blend(weights, values)
        combined_ref[rows, :] = (attended + context_ref[rows, :]).astype(BF16)
        yield True

    def feed_forward(part):
        columns = pl.ds(part * PAIR * side, PAIR * side)
        image = regions_of(image_ref[:, columns, :].astype(F32), side)
        combined = previous[part * chunk : (part + 1) * chunk]
        residual = image + jnp.dot(combined, out_weight_ref[...], preferred_element_type=F32)
        yield True
        stored = residual.astype(BF16).astype(F32)
        second = normalize(stored, gain_ref[...]).astype(BF16)
        yield True
        lifted = jnp.dot(second, up_ref[...], preferred_element_type=F32)
        yield True
        hidden = gelu(lifted).astype(BF16)
        yield True
        refined = stored + jnp.dot(hidden, down_ref[...], preferred_element_type=F32)
        result_ref[:, columns, :] = strip_of(refined, side, PAIR * side).astype(BF16)
        yield True

    lines = [feed_forward(part) for part in range(batch // PAIR)]
    lines += [attention(region) for region in range(batch)]
    while lines:
        lines = [line for line in lines if next(line, None) is not None]


def tail(position, early, fetched, late, queries, context, image, weights, side, picks):
    height, width, channels = image.shape
    area = side * side
    per_row = width // side
    batch = math.gcd(per_row, 4)
    halves = per_row // batch
    steps = height // side * halves
    full = lambda a: pl.BlockSpec(a.shape, lambda i, position: (0,) * a.ndim)
    now = lambda i: jnp.minimum(i, steps - 1)
    before = lambda i: jnp.maximum(i - 1, 0)
    tokens = pl.BlockSpec((batch * area, channels), lambda i, position: (now(i), 0))
    strip = pl.BlockSpec(
        (side, batch * side, channels),
        lambda i, position: (before(i) // halves, before(i) % halves, 0),
    )
    regions = pl.BlockSpec((batch * picks, area, channels), lambda i, position: (now(i), 0, 0))
    total = sum(a.shape[0] for a in late)
    return pl.pallas_call(
        functools.partial(tail_kernel, side, picks, batch, early, len(late)),
        grid_spec=pltpu.PrefetchScalarGridSpec(
            num_scalar_prefetch=1,
            grid=(steps + 1,),
            in_specs=[pl.BlockSpec(memory_space=pl.ANY)] * len(late)
            + [regions, tokens, tokens, strip]
            + [full(w) for w in weights],
            out_specs=strip,
            scratch_shapes=[
                pltpu.VMEM((total, area, channels), BF16),
                pltpu.VMEM((batch * area, channels), BF16),
                pltpu.SemaphoreType.DMA((len(late),)),
            ],
        ),
        out_shape=jax.ShapeDtypeStruct(image.shape, BF16),
        cost_estimate=pl.CostEstimate(
            flops=image.size * 4000, bytes_accessed=16 * image.size, transcendentals=40 * image.size
        ),
        name="tail",
    )(position, *late, fetched, queries, context, image, *weights)


def layer_blocks(block, layer, layers):
    if layers != 4:
        return [block] + [
            lax.ppermute(block, "z", [(i, i ^ step) for i in range(layers)])
            for step in range(1, layers)
        ]

    def hop(block, pairs):
        return lax.ppermute(block, "z", pairs)

    beside = hop(block, [(0, 1), (1, 0), (2, 3), (3, 2)])
    middle = hop(block, [(1, 2), (2, 1)])
    middle_two = hop(beside, [(1, 2), (2, 1)])
    ends_two = hop(middle, [(1, 0), (2, 3)])
    ends_three = hop(middle_two, [(1, 0), (2, 3)])
    inside = (layer == 1) | (layer == 2)
    return [
        block,
        beside,
        jnp.where(inside, middle_two, ends_two),
        jnp.where(inside, middle, ends_three),
    ]


def block(
    image, routes, norm_gain, qkv_weight, lce_weight, out_weight, mlp_gain, up_weight, down_weight
):
    height, _, channels = image.shape
    layers, across = lax.axis_size("z"), lax.axis_size("x")
    peers = lax.axis_size("rows") * across
    devices = peers * layers
    region_rows, region_cols, pick_count = routes.shape
    side = height // region_rows
    pair_count = region_rows * region_cols * pick_count
    capacity = max(2, 2 * pair_count // devices)
    all_cols = region_cols * layers * across

    regions = region_rows * region_cols
    peer = lax.axis_index("rows") * across + lax.axis_index("x")
    layer = lax.axis_index("z")
    here = jnp.stack([peer, layer])

    targets = routes.reshape(pair_count)
    target_row = targets // all_cols
    target_col = targets % all_cols
    owner_col = target_col // region_cols
    owner_layer = owner_col // across
    owner_peer = target_row // region_rows * across + owner_col % across
    local_index = target_row % region_rows * region_cols + target_col % region_cols
    owners = owner_peer * layers + owner_layer
    pairs = jnp.arange(pair_count, dtype=jnp.int32)
    earlier = (owners[:, None] == owners[None, :]) & (pairs[None, :] < pairs[:, None])
    slot = jnp.sum(earlier.astype(jnp.int32), axis=1)
    distance = owner_peer ^ peer
    chunk = owner_layer ^ layer
    groups = [(0, 1), *((step,) for step in range(2, layers))]
    position, start = jnp.zeros_like(slot), 0
    for members in groups:
        replies = start + len(members) * regions
        for place, step in enumerate(members):
            here_at = start + place * regions + local_index
            sent_at = (
                replies + ((distance - 1) * len(members) + place) * capacity + slot
            )
            position = jnp.where(
                chunk == step, jnp.where(distance == 0, here_at, sent_at), position
            )
        early = start
        start = replies + (peers - 1) * len(members) * capacity
    asked = owners * capacity + slot
    slots = jnp.arange(devices * capacity, dtype=jnp.int32)
    requests = jnp.sum(
        jnp.where(asked[None, :] == slots[:, None], local_index[None, :], 0), axis=1
    )
    wanted = lax.all_to_all(
        requests.reshape(peers, layers * capacity), ("rows", "x"), 0, 0, tiled=True
    ).reshape(-1)

    normed = norm_regions(image, norm_gain, side)

    held = layer_blocks(normed, layer, layers)
    arrived = []
    for members in groups:
        sources = [held[step] for step in members]
        packed = pack(sources, here, wanted, members, peers, layers, capacity)
        arrived.append(
            sources
            + [
                lax.ppermute(part, ("rows", "x"), [(i, i ^ far) for i in range(peers)])
                for far, part in enumerate(packed, 1)
            ]
        )
    late = arrived.pop()
    fetched = collect(position, sum(arrived, []), math.gcd(pair_count, 8))

    margin = (lce_weight.shape[0] - 1) // 2
    around = halo(image, margin, 8)
    context, queries = context_and_queries(
        image, around, norm_gain, qkv_weight, lce_weight, side, margin
    )
    weights = (
        qkv_weight,
        out_weight,
        mlp_gain.reshape(1, channels),
        up_weight,
        down_weight,
    )
    return tail(position, early, fetched, late, queries, context, image, weights, side, pick_count)


def solution(mesh):
    devices = mesh.devices
    layers = len({device.coords[2] for device in devices[0]})
    split = Mesh(
        devices.reshape(devices.shape[0], layers, devices.shape[1] // layers), ("rows", "z", "x")
    )
    grid = P("rows", ("z", "x"), None)
    in_specs = (grid, grid, P(), P(), P(), P(), P(), P(), P())
    return jax.shard_map(block, mesh=split, in_specs=in_specs, out_specs=grid, check_vma=False)
```

```python
import functools
import math

import jax
import jax.numpy as jnp
from jax import lax
from jax.experimental import pallas as pl
from jax.experimental.pallas import tpu as pltpu
from jax.sharding import Mesh
from jax.sharding import PartitionSpec as P

HEADS = 4
PAIR = 2
EPSILON = 1e-06
F32 = jnp.float32
BF16 = jnp.bfloat16


def from_sides(low, high, axis):
    count = math.prod(lax.axis_size(name) for name in (axis if isinstance(axis, tuple) else (axis,)))
    forward = [(i, i + 1) for i in range(count - 1)]
    backward = [(target, source) for source, target in forward]
    return lax.ppermute(high, axis, forward), lax.ppermute(low, axis, backward)


def halo(top, bottom, left, right):
    border = left.shape[1]
    above, below = from_sides(top, bottom, "rows")
    low = jnp.concatenate([above[:, :border], left, below[:, :border]], axis=0)
    high = jnp.concatenate([above[:, -border:], right, below[:, -border:]], axis=0)
    left, right = from_sides(low, high, ("z", "x"))
    return above, below, left, right


def normalize(floats, gain):
    centered = floats - jnp.mean(floats, axis=-1, keepdims=True)
    spread = jnp.mean(centered * centered, axis=-1, keepdims=True)
    return centered * lax.rsqrt(spread + EPSILON) * gain


def regions_of(strip, side):
    height, width, channels = strip.shape
    return (
        strip.reshape(height, width // side, side, channels)
        .transpose(1, 0, 2, 3)
        .reshape(height * width, channels)
    )


def strip_of(tokens, side, width):
    channels = tokens.shape[-1]
    return (
        tokens.reshape(width // side, side, side, channels)
        .transpose(1, 0, 2, 3)
        .reshape(side, width, channels)
    )


def norm_kernel(side, image_ref, gain_ref, out_ref, top_ref, bottom_ref, left_ref, right_ref):
    step = pl.program_id(0)
    tokens = image_ref[...]
    normed = normalize(tokens.astype(F32), gain_ref[...])
    out_ref[...] = regions_of(normed, side).astype(BF16).reshape(out_ref.shape)
    margin, width, border = top_ref.shape[0], tokens.shape[1], left_ref.shape[1]
    left_ref[...] = image_ref[:, pl.ds(0, border), :]
    right_ref[...] = image_ref[:, pl.ds(width - border, border), :]

    @pl.when(step == 0)
    def _():
        top_ref[...] = image_ref[pl.ds(0, margin)]

    @pl.when(step == pl.num_programs(0) - 1)
    def _():
        bottom_ref[...] = image_ref[pl.ds(side - margin, margin)]


def norm_regions(image, gain, side, margin, border):
    height, width, channels = image.shape
    per_row = width // side
    edge = jax.ShapeDtypeStruct((margin, width, channels), BF16)
    flank = jax.ShapeDtypeStruct((height, border, channels), BF16)
    return pl.pallas_call(
        functools.partial(norm_kernel, side),
        grid=(height // side,),
        in_specs=[
            pl.BlockSpec((side, width, channels), lambda i: (i, 0, 0)),
            pl.BlockSpec((1, channels), lambda i: (0, 0)),
        ],
        out_specs=[
            pl.BlockSpec((per_row, side * side, channels), lambda i: (i, 0, 0)),
            pl.BlockSpec(edge.shape, lambda i: (0, 0, 0)),
            pl.BlockSpec(edge.shape, lambda i: (0, 0, 0)),
            pl.BlockSpec((side, border, channels), lambda i: (i, 0, 0)),
            pl.BlockSpec((side, border, channels), lambda i: (i, 0, 0)),
        ],
        out_shape=[
            jax.ShapeDtypeStruct((height // side * per_row, side * side, channels), BF16),
            edge,
            edge,
            flank,
            flank,
        ],
        cost_estimate=pl.CostEstimate(
            flops=10 * image.size, bytes_accessed=4 * image.size, transcendentals=0
        ),
        name="norm_regions",
    )(image, gain.reshape(1, channels))


def context_kernel(
    side,
    margin,
    image_ref,
    above_ref,
    below_ref,
    left_ref,
    right_ref,
    gain_ref,
    weight_ref,
    lce_ref,
    context_ref,
    query_ref,
    padded,
):
    step = pl.program_id(0)
    height, width, channels = image_ref.shape
    border = left_ref.shape[1]

    @pl.when(step == 0)
    def _():
        inner = pl.ds(border, width)
        padded[:margin, inner] = above_ref[...].astype(F32)
        padded[pl.ds(margin, height), inner] = image_ref[...].astype(F32)
        padded[pl.ds(margin + height, margin), inner] = below_ref[...].astype(F32)
        padded[:, :border] = left_ref[...].astype(F32)
        padded[:, pl.ds(border + width, border)] = right_ref[...].astype(F32)

    rows = side + 2 * margin
    strip = padded[pl.ds(step * side, rows)]
    wide = strip.shape[1]
    normed = normalize(strip, gain_ref[...]).astype(BF16).reshape(rows * wide, channels)
    weight = jnp.concatenate([weight_ref[:, :channels], weight_ref[:, 2 * channels :]], axis=1)
    projected = jnp.dot(normed, weight, preferred_element_type=F32).astype(BF16)
    values = projected[:, channels:].astype(F32).reshape(rows, wide, channels)
    summed = jnp.zeros((side, width, channels), F32)
    for col in range(2 * margin + 1):
        moved = pltpu.roll(values, wide - (border - margin + col), 1)[:, :width]
        for row in range(2 * margin + 1):
            summed = summed + moved[row : row + side] * lce_ref[row, pl.ds(col, 1), :]
    context_ref[...] = regions_of(summed, side)
    queries = projected[:, :channels].astype(F32).reshape(rows, wide, channels)
    inner = queries[margin : margin + side, border : border + width]
    query_ref[...] = regions_of(inner, side).astype(BF16)


def context_and_queries(image, around, gain, qkv_weight, lce_weight, side, margin):
    height, width, channels = image.shape
    border = around[-1].shape[1]
    tokens = height * width
    full = lambda a: pl.BlockSpec(a.shape, lambda i: (0,) * a.ndim)
    operands = (image, *around, gain.reshape(1, channels), qkv_weight, lce_weight)
    return pl.pallas_call(
        functools.partial(context_kernel, side, margin),
        grid=(height // side,),
        in_specs=[full(a) for a in operands],
        out_specs=[
            pl.BlockSpec((side * width, channels), lambda i: (i, 0)),
            pl.BlockSpec((side * width, channels), lambda i: (i, 0)),
        ],
        out_shape=[
            jax.ShapeDtypeStruct((tokens, channels), F32),
            jax.ShapeDtypeStruct((tokens, channels), BF16),
        ],
        scratch_shapes=[
            pltpu.VMEM((height + 2 * margin, width + 2 * border, channels), F32),
        ],
        cost_estimate=pl.CostEstimate(
            flops=tokens * channels * 600, bytes_accessed=10 * tokens * channels, transcendentals=0
        ),
        name="context",
    )(*operands)


def is_inside(layer):
    return (layer == 1) | (layer == 2)


def pack_kernel(chunks, capacity, joint, place_of, wanted_ref, *refs):
    peer, layer = place_of()
    count = sum(options for _, options in chunks)
    sources, out_refs = refs[:count], refs[count:]
    distances = range(1, out_refs[0].shape[0] if joint else len(out_refs) + 1)
    inside = is_inside(layer)

    def fill(source_ref, chunk, place):
        for distance in distances:
            other = peer ^ distance
            for slot in range(capacity):
                region = source_ref[wanted_ref[other, 0, (layer ^ chunk) * capacity + slot]]
                if joint:
                    out_refs[0][other, place * capacity + slot] = region
                else:
                    out_refs[distance - 1][place * capacity + slot] = region

    at = 0
    for place, (chunk, options) in enumerate(chunks):
        if options == 1:
            fill(sources[at], chunk, place)
        else:
            pl.when(inside)(functools.partial(fill, sources[at], chunk, place))
            pl.when(~inside)(functools.partial(fill, sources[at + 1], chunk, place))
        at += options


def pack(chunks, place_of, wanted, peers, capacity, joint):
    sources = sum(chunks.values(), [])
    tile = sources[0].shape
    shape = (capacity * len(chunks), *tile[1:])
    shapes = [(peers, *shape)] if joint else [shape] * (peers - 1)
    return pl.pallas_call(
        functools.partial(
            pack_kernel, tuple((k, len(v)) for k, v in chunks.items()), capacity, joint, place_of
        ),
        in_specs=[pl.BlockSpec(memory_space=pltpu.SMEM)]
        + [pl.BlockSpec(memory_space=pltpu.VMEM)] * len(sources),
        out_specs=[pl.BlockSpec(memory_space=pltpu.VMEM)] * len(shapes),
        out_shape=[jax.ShapeDtypeStruct(a, BF16) for a in shapes],
        cost_estimate=pl.CostEstimate(
            flops=0, bytes_accessed=4 * peers * math.prod(shape), transcendentals=0
        ),
        name="pack",
    )(wanted, *sources)


def load_all(options, sources, landed, sems, layer):
    waits, start, at = [], 0, 0
    inside = is_inside(layer)
    for i, count in enumerate(options):
        size = sources[at].shape[0]
        copies = [
            pltpu.make_async_copy(source, landed.at[pl.ds(start, size)], sems.at[i])
            for source in sources[at : at + count]
        ]
        if count == 1:
            copies[0].start()
        else:
            pl.when(inside)(copies[0].start)
            pl.when(~inside)(copies[1].start)
        waits.append(copies[0])
        start += size
        at += count
    for copy in waits:
        copy.wait()


def rows_of(sources):
    return sum(options[0].shape[0] for options in sources)


def collect_kernel(options, place_of, position_ref, *refs):
    sources, out_ref, landed, sems = refs[: sum(options)], refs[-3], refs[-2], refs[-1]
    step = pl.program_id(0)

    @pl.when(step == 0)
    def _():
        load_all(options, sources, landed, sems, place_of()[1])

    total = landed.shape[0]
    per_step = out_ref.shape[0]
    for i in range(per_step):
        at = position_ref[step * per_step + i]
        out_ref[i] = landed[jnp.where(at < total, at, 0)]


def collect(position, sources, place_of, steps):
    shape = sources[0][0].shape[1:]
    total = rows_of(sources)
    pairs = position.shape[0]
    flat = sum(sources, [])
    return pl.pallas_call(
        functools.partial(collect_kernel, tuple(map(len, sources)), place_of),
        grid_spec=pltpu.PrefetchScalarGridSpec(
            num_scalar_prefetch=1,
            grid=(steps,),
            in_specs=[pl.BlockSpec(memory_space=pl.ANY)] * len(flat),
            out_specs=pl.BlockSpec((pairs // steps, *shape), lambda i, _: (i, 0, 0)),
            scratch_shapes=[
                pltpu.VMEM((total, *shape), BF16),
                pltpu.SemaphoreType.DMA((len(sources),)),
            ],
        ),
        out_shape=jax.ShapeDtypeStruct((pairs, *shape), BF16),
        cost_estimate=pl.CostEstimate(
            flops=0, bytes_accessed=2 * (total + pairs) * math.prod(shape), transcendentals=0
        ),
        name="collect",
    )(position, *flat)


def project(fetched, weight_ref):
    channels = fetched.shape[-1]
    projected = jnp.dot(
        fetched, weight_ref[:, channels : 3 * channels], preferred_element_type=F32
    ).astype(BF16)
    return projected[:, :channels], projected[:, channels:]


def score(queries, keys):
    area, channels = queries.shape
    lane = lax.broadcasted_iota(jnp.int32, (area, channels), 1) // (channels // HEADS)
    zero = jnp.zeros_like(queries)
    stacked = jnp.concatenate(
        [jnp.where(lane == head, queries, zero) for head in range(HEADS)], axis=0
    )
    return lax.dot_general(
        stacked, keys, (((1,), (1,)), ((), ())), preferred_element_type=F32
    )


def blend(weights, values):
    area, channels = weights.shape[0] // HEADS, values.shape[1]
    blended = jnp.dot(weights, values, preferred_element_type=F32)
    lane = lax.broadcasted_iota(jnp.int32, (area, channels), 1) // (channels // HEADS)
    picked = blended[:area]
    for head in range(1, HEADS):
        picked = jnp.where(lane == head, blended[head * area : (head + 1) * area], picked)
    return picked


def gelu(lifted):
    inner = lifted * (0.7978845608028654 + 0.035677408136300125 * (lifted * lifted))
    return lifted * (0.5 + 0.5 * jnp.tanh(inner))


def tail_kernel(side, picks, batch, early, options, place_of, position_ref, *refs):
    late_count = sum(options)
    late = refs[:late_count]
    (
        fetched_ref,
        query_ref,
        context_ref,
        image_ref,
        qkv_ref,
        out_weight_ref,
        gain_ref,
        up_ref,
        down_ref,
        result_ref,
        landed,
        combined_ref,
        sems,
    ) = refs[late_count:]
    step = pl.program_id(0)
    last = pl.num_programs(0) - 2

    @pl.when(step == 0)
    def _():
        combined_ref[...] = jnp.zeros_like(combined_ref)
        load_all(options, late, landed, sems, place_of()[1])

    area, channels = fetched_ref.shape[1:]
    exponent = (channels // HEADS) ** (-0.5) * math.log2(math.e)
    first = jnp.minimum(step, last) * (batch * picks)

    def piece(which):
        at = position_ref[first + which]
        is_late = at >= early
        return jnp.where(is_late, landed[jnp.where(is_late, at - early, 0)], fetched_ref[which])

    previous = combined_ref[...]
    chunk = PAIR * area

    def attention(region):
        rows = pl.ds(region * area, area)
        fetched = jnp.concatenate(
            [piece(which) for which in range(region * picks, (region + 1) * picks)], axis=0
        )
        keys, values = project(fetched, qkv_ref)
        yield True
        scores = score(query_ref[rows, :], keys)
        yield True
        highest = jnp.max(scores, axis=-1, keepdims=True)
        expons = jnp.exp2((scores - highest) * exponent)
        yield True
        total = jnp.sum(expons, axis=-1, keepdims=True)
        weights = (expons * (1.0 / total)).astype(BF16)
        yield True
        attended = blend(weights, values)
        combined_ref[rows, :] = (attended + context_ref[rows, :]).astype(BF16)
        yield True

    def feed_forward(part):
        columns = pl.ds(part * PAIR * side, PAIR * side)
        image = regions_of(image_ref[:, columns, :].astype(F32), side)
        combined = previous[part * chunk : (part + 1) * chunk]
        residual = image + jnp.dot(combined, out_weight_ref[...], preferred_element_type=F32)
        yield True
        stored = residual.astype(BF16).astype(F32)
        second = normalize(stored, gain_ref[...]).astype(BF16)
        yield True
        lifted = jnp.dot(second, up_ref[...], preferred_element_type=F32)
        yield True
        hidden = gelu(lifted).astype(BF16)
        yield True
        refined = stored + jnp.dot(hidden, down_ref[...], preferred_element_type=F32)
        result_ref[:, columns, :] = strip_of(refined, side, PAIR * side).astype(BF16)
        yield True

    lines = [feed_forward(part) for part in range(batch // PAIR)]
    lines += [attention(region) for region in range(batch)]
    while lines:
        lines = [line for line in lines if next(line, None) is not None]


def tail(position, early, fetched, late, place_of, queries, context, image, weights, side, picks):
    height, width, channels = image.shape
    area = side * side
    per_row = width // side
    batch = math.gcd(per_row, 4)
    halves = per_row // batch
    steps = height // side * halves
    full = lambda a: pl.BlockSpec(a.shape, lambda i, position: (0,) * a.ndim)
    now = lambda i: jnp.minimum(i, steps - 1)
    before = lambda i: jnp.maximum(i - 1, 0)
    tokens = pl.BlockSpec((batch * area, channels), lambda i, position: (now(i), 0))
    strip = pl.BlockSpec(
        (side, batch * side, channels),
        lambda i, position: (before(i) // halves, before(i) % halves, 0),
    )
    regions = pl.BlockSpec((batch * picks, area, channels), lambda i, position: (now(i), 0, 0))
    total = rows_of(late)
    flat = sum(late, [])
    return pl.pallas_call(
        functools.partial(
            tail_kernel, side, picks, batch, early, tuple(map(len, late)), place_of
        ),
        grid_spec=pltpu.PrefetchScalarGridSpec(
            num_scalar_prefetch=1,
            grid=(steps + 1,),
            in_specs=[pl.BlockSpec(memory_space=pl.ANY)] * len(flat)
            + [regions, tokens, tokens, strip]
            + [full(w) for w in weights],
            out_specs=strip,
            scratch_shapes=[
                pltpu.VMEM((total, area, channels), BF16),
                pltpu.VMEM((batch * area, channels), BF16),
                pltpu.SemaphoreType.DMA((len(late),)),
            ],
        ),
        out_shape=jax.ShapeDtypeStruct(image.shape, BF16),
        cost_estimate=pl.CostEstimate(
            flops=image.size * 4000, bytes_accessed=16 * image.size, transcendentals=40 * image.size
        ),
        name="tail",
    )(position, *flat, fetched, queries, context, image, *weights)


def layer_blocks(block, layers):
    if layers != 4:
        return [[block]] + [
            [lax.ppermute(block, "z", [(i, i ^ step) for i in range(layers)])]
            for step in range(1, layers)
        ]

    def hop(block, pairs):
        return lax.ppermute(block, "z", pairs)

    beside = hop(block, [(0, 1), (1, 0), (2, 3), (3, 2)])
    middle = hop(block, [(1, 2), (2, 1)])
    middle_two = hop(beside, [(1, 2), (2, 1)])
    ends_two = hop(middle, [(1, 0), (2, 3)])
    ends_three = hop(middle_two, [(1, 0), (2, 3)])
    return [[block], [beside], [middle_two, ends_two], [middle, ends_three]]


def block(
    image, routes, norm_gain, qkv_weight, lce_weight, out_weight, mlp_gain, up_weight, down_weight
):
    height, _, channels = image.shape
    layers, across = lax.axis_size("z"), lax.axis_size("x")
    peers = lax.axis_size("rows") * across
    devices = peers * layers
    region_rows, region_cols, pick_count = routes.shape
    side = height // region_rows
    pair_count = region_rows * region_cols * pick_count
    capacity = max(2, 2 * pair_count // devices)
    all_cols = region_cols * layers * across

    regions = region_rows * region_cols

    def place_of():
        return lax.axis_index("rows") * across + lax.axis_index("x"), lax.axis_index("z")

    peer, layer = place_of()

    targets = routes.reshape(pair_count)
    target_row = targets // all_cols
    target_col = targets % all_cols
    owner_col = target_col // region_cols
    owner_layer = owner_col // across
    owner_peer = target_row // region_rows * across + owner_col % across
    local_index = target_row % region_rows * region_cols + target_col % region_cols
    owners = owner_peer * layers + owner_layer
    pairs = jnp.arange(pair_count, dtype=jnp.int32)
    earlier = (owners[:, None] == owners[None, :]) & (pairs[None, :] < pairs[:, None])
    slot = jnp.sum(earlier.astype(jnp.int32), axis=1)
    distance = owner_peer ^ peer
    chunk = owner_layer ^ layer
    groups = [(0, 1), *((step,) for step in range(2, layers))]
    position, start = jnp.zeros_like(slot), 0
    for number, members in enumerate(groups):
        joint = number == 0
        replies = start + len(members) * regions
        sender = owner_peer if joint else distance - 1
        for place, step in enumerate(members):
            here_at = start + place * regions + local_index
            sent_at = replies + (sender * len(members) + place) * capacity + slot
            position = jnp.where(
                chunk == step, jnp.where(distance == 0, here_at, sent_at), position
            )
        early = start
        start = replies + (peers - 1 + joint) * len(members) * capacity
    lanes = -(-layers * capacity // 128) * 128
    asked = owner_peer * lanes + owner_layer * capacity + slot
    slots = jnp.arange(peers * lanes, dtype=jnp.int32)
    requests = jnp.sum(
        jnp.where(asked[None, :] == slots[:, None], local_index[None, :], 0), axis=1
    )
    wanted = lax.all_to_all(
        requests.reshape(peers, 1, lanes), ("rows", "x"), 0, 0, tiled=True
    )

    margin = (lce_weight.shape[0] - 1) // 2
    normed, *edges = norm_regions(image, norm_gain, side, margin, 8)

    held = layer_blocks(normed, layers)
    arrived = []
    for number, members in enumerate(groups):
        chunks = {step: held[step] for step in members}
        joint = number == 0
        packed = pack(chunks, place_of, wanted, peers, capacity, joint)
        if joint:
            got = lax.all_to_all(packed[0], ("rows", "x"), 0, 0, tiled=True)
            got = [got.reshape(-1, *normed.shape[1:])]
        else:
            got = [
                lax.ppermute(part, ("rows", "x"), [(i, i ^ far) for i in range(peers)])
                for far, part in enumerate(packed, 1)
            ]
        arrived.append([*chunks.values(), *([part] for part in got)])
    late = arrived.pop()
    fetched = collect(position, sum(arrived, []), place_of, math.gcd(pair_count, 8))

    around = halo(*edges)
    context, queries = context_and_queries(
        image, around, norm_gain, qkv_weight, lce_weight, side, margin
    )
    weights = (
        qkv_weight,
        out_weight,
        mlp_gain.reshape(1, channels),
        up_weight,
        down_weight,
    )
    return tail(position, early, fetched, late, place_of, queries, context, image, weights, side, pick_count)


def solution(mesh):
    devices = mesh.devices
    layers = len({device.coords[2] for device in devices[0]})
    split = Mesh(
        devices.reshape(devices.shape[0], layers, devices.shape[1] // layers), ("rows", "z", "x")
    )
    grid = P("rows", ("z", "x"), None)
    in_specs = (grid, grid, P(), P(), P(), P(), P(), P(), P())
    return jax.shard_map(block, mesh=split, in_specs=in_specs, out_specs=grid, check_vma=False)
```

```python
import functools
import math

import jax
import jax.numpy as jnp
from jax import lax
from jax.experimental import pallas as pl
from jax.experimental.pallas import tpu as pltpu
from jax.sharding import Mesh
from jax.sharding import PartitionSpec as P

HEADS = 4
PAIR = 2
EPSILON = 1e-06
F32 = jnp.float32
BF16 = jnp.bfloat16


def from_sides(low, high, axis):
    count = math.prod(lax.axis_size(name) for name in (axis if isinstance(axis, tuple) else (axis,)))
    forward = [(i, i + 1) for i in range(count - 1)]
    backward = [(target, source) for source, target in forward]
    return lax.ppermute(high, axis, forward), lax.ppermute(low, axis, backward)


def normalize(floats, gain):
    centered = floats - jnp.mean(floats, axis=-1, keepdims=True)
    spread = jnp.mean(centered * centered, axis=-1, keepdims=True)
    return centered * lax.rsqrt(spread + EPSILON) * gain


def regions_of(strip, side):
    height, width, channels = strip.shape
    return (
        strip.reshape(height, width // side, side, channels)
        .transpose(1, 0, 2, 3)
        .reshape(height * width, channels)
    )


def strip_of(tokens, side, width):
    channels = tokens.shape[-1]
    return (
        tokens.reshape(width // side, side, side, channels)
        .transpose(1, 0, 2, 3)
        .reshape(side, width, channels)
    )


def norm_kernel(side, image_ref, gain_ref, out_ref, top_ref, bottom_ref, left_ref, right_ref):
    step = pl.program_id(0)
    tokens = image_ref[...]
    normed = normalize(tokens.astype(F32), gain_ref[...])
    out_ref[...] = regions_of(normed, side).astype(BF16).reshape(out_ref.shape)
    margin, width, border = top_ref.shape[0], tokens.shape[1], left_ref.shape[1]
    left_ref[...] = image_ref[:, pl.ds(0, border), :]
    right_ref[...] = image_ref[:, pl.ds(width - border, border), :]

    @pl.when(step == 0)
    def _():
        top_ref[...] = image_ref[pl.ds(0, margin)]

    @pl.when(step == pl.num_programs(0) - 1)
    def _():
        bottom_ref[...] = image_ref[pl.ds(side - margin, margin)]


def norm_regions(image, gain, side, margin, border):
    height, width, channels = image.shape
    per_row = width // side
    edge = jax.ShapeDtypeStruct((margin, width, channels), BF16)
    flank = jax.ShapeDtypeStruct((height, border, channels), BF16)
    return pl.pallas_call(
        functools.partial(norm_kernel, side),
        grid=(height // side,),
        in_specs=[
            pl.BlockSpec((side, width, channels), lambda i: (i, 0, 0)),
            pl.BlockSpec((1, channels), lambda i: (0, 0)),
        ],
        out_specs=[
            pl.BlockSpec((per_row, side * side, channels), lambda i: (i, 0, 0)),
            pl.BlockSpec(edge.shape, lambda i: (0, 0, 0)),
            pl.BlockSpec(edge.shape, lambda i: (0, 0, 0)),
            pl.BlockSpec((side, border, channels), lambda i: (i, 0, 0)),
            pl.BlockSpec((side, border, channels), lambda i: (i, 0, 0)),
        ],
        out_shape=[
            jax.ShapeDtypeStruct((height // side * per_row, side * side, channels), BF16),
            edge,
            edge,
            flank,
            flank,
        ],
        cost_estimate=pl.CostEstimate(
            flops=10 * image.size, bytes_accessed=4 * image.size, transcendentals=0
        ),
        name="norm_regions",
    )(image, gain.reshape(1, channels))


def context_kernel(
    side,
    margin,
    image_ref,
    above_ref,
    below_ref,
    left_ref,
    right_ref,
    gain_ref,
    weight_ref,
    lce_ref,
    context_ref,
    query_ref,
    padded,
):
    step = pl.program_id(0)
    height, width, channels = image_ref.shape
    border = left_ref.shape[1]

    @pl.when(step == 0)
    def _():
        inner = pl.ds(border, width)
        padded[:margin, inner] = above_ref[...].astype(F32)
        padded[pl.ds(margin, height), inner] = image_ref[...].astype(F32)
        padded[pl.ds(margin + height, margin), inner] = below_ref[...].astype(F32)
        padded[:, :border] = left_ref[...].astype(F32)
        padded[:, pl.ds(border + width, border)] = right_ref[...].astype(F32)

    rows = side + 2 * margin
    strip = padded[pl.ds(step * side, rows)]
    wide = strip.shape[1]
    normed = normalize(strip, gain_ref[...]).astype(BF16).reshape(rows * wide, channels)
    weight = jnp.concatenate([weight_ref[:, :channels], weight_ref[:, 2 * channels :]], axis=1)
    projected = jnp.dot(normed, weight, preferred_element_type=F32).astype(BF16)
    values = projected[:, channels:].astype(F32).reshape(rows, wide, channels)
    summed = jnp.zeros((side, width, channels), F32)
    for col in range(2 * margin + 1):
        moved = pltpu.roll(values, wide - (border - margin + col), 1)[:, :width]
        for row in range(2 * margin + 1):
            summed = summed + moved[row : row + side] * lce_ref[row, pl.ds(col, 1), :]
    context_ref[...] = regions_of(summed, side)
    queries = projected[:, :channels].astype(F32).reshape(rows, wide, channels)
    inner = queries[margin : margin + side, border : border + width]
    query_ref[...] = regions_of(inner, side).astype(BF16)


def context_and_queries(image, around, gain, qkv_weight, lce_weight, side, margin):
    height, width, channels = image.shape
    border = around[-1].shape[1]
    tokens = height * width
    full = lambda a: pl.BlockSpec(a.shape, lambda i: (0,) * a.ndim)
    operands = (image, *around, gain.reshape(1, channels), qkv_weight, lce_weight)
    return pl.pallas_call(
        functools.partial(context_kernel, side, margin),
        grid=(height // side,),
        in_specs=[full(a) for a in operands],
        out_specs=[
            pl.BlockSpec((side * width, channels), lambda i: (i, 0)),
            pl.BlockSpec((side * width, channels), lambda i: (i, 0)),
        ],
        out_shape=[
            jax.ShapeDtypeStruct((tokens, channels), F32),
            jax.ShapeDtypeStruct((tokens, channels), BF16),
        ],
        scratch_shapes=[
            pltpu.VMEM((height + 2 * margin, width + 2 * border, channels), F32),
        ],
        cost_estimate=pl.CostEstimate(
            flops=tokens * channels * 600, bytes_accessed=10 * tokens * channels, transcendentals=0
        ),
        name="context",
    )(*operands)


def is_inside(layer):
    return (layer == 1) | (layer == 2)


def frame_kernel(above_ref, below_ref, left_ref, right_ref, low_ref, high_ref):
    margin, width = above_ref.shape[:2]
    height, border = left_ref.shape[:2]
    for out_ref, flank_ref, first in ((low_ref, left_ref, 0), (high_ref, right_ref, width - border)):
        out_ref[pl.ds(0, margin)] = above_ref[:, pl.ds(first, border), :]
        out_ref[pl.ds(margin, height)] = flank_ref[...]
        out_ref[pl.ds(margin + height, margin)] = below_ref[:, pl.ds(first, border), :]


def pack_kernel(jobs, options, outputs, framed, capacity, layers, place_of, wanted_ref, *refs):
    peer, layer = place_of()
    sources = refs[: sum(options)]
    outs = refs[len(refs) - outputs :]
    if framed:
        frame_kernel(*refs[sum(options) : sum(options) + 4], *outs[-2:])
    inside = is_inside(layer)

    def fill(source_ref, out_ref, place, distance, column):
        other = peer ^ distance
        base = ((layer ^ column) if column < layers else column) * capacity
        for slot in range(capacity):
            region = source_ref[wanted_ref[other, 0, base + slot]]
            if place is None:
                out_ref[other, slot] = region
            else:
                out_ref[place * capacity + slot] = region

    def fill_all(shift, chosen):
        for out, place, source, distance, column in chosen:
            at = sum(options[:source]) + shift
            fill(sources[at], outs[out], place, distance, column)

    fill_all(0, [job for job in jobs if options[job[2]] == 1])
    paired = [job for job in jobs if options[job[2]] == 2]
    if paired:
        pl.when(inside)(functools.partial(fill_all, 0, paired))
        pl.when(~inside)(functools.partial(fill_all, 1, paired))


def pack(jobs, shapes, sources, place_of, wanted, capacity, layers, frame=()):
    flat = sum(sources, [])
    if frame:
        margin, (height, border, channels) = frame[0].shape[0], frame[2].shape
        shapes = shapes + [(height + 2 * margin, border, channels)] * 2
    in_vmem = pl.BlockSpec(memory_space=pltpu.VMEM)
    return pl.pallas_call(
        functools.partial(
            pack_kernel,
            tuple(jobs),
            tuple(map(len, sources)),
            len(shapes),
            len(frame) > 0,
            capacity,
            layers,
            place_of,
        ),
        in_specs=[pl.BlockSpec(memory_space=pltpu.SMEM)] + [in_vmem] * (len(flat) + len(frame)),
        out_specs=[in_vmem] * len(shapes),
        out_shape=[jax.ShapeDtypeStruct(a, BF16) for a in shapes],
        cost_estimate=pl.CostEstimate(
            flops=0, bytes_accessed=4 * sum(map(math.prod, shapes)), transcendentals=0
        ),
        name="pack",
    )(wanted, *flat, *frame)


def load_all(options, sources, landed, sems, layer):
    waits, start, at = [], 0, 0
    inside = is_inside(layer)
    for i, count in enumerate(options):
        size = sources[at].shape[0]
        copies = [
            pltpu.make_async_copy(source, landed.at[pl.ds(start, size)], sems.at[i])
            for source in sources[at : at + count]
        ]
        if count == 1:
            copies[0].start()
        else:
            pl.when(inside)(copies[0].start)
            pl.when(~inside)(copies[1].start)
        waits.append(copies[0])
        start += size
        at += count
    for copy in waits:
        copy.wait()


def rows_of(sources):
    return sum(options[0].shape[0] for options in sources)


def collect_kernel(options, place_of, position_ref, *refs):
    sources, out_ref, landed, sems = refs[: sum(options)], refs[-3], refs[-2], refs[-1]
    step = pl.program_id(0)

    @pl.when(step == 0)
    def _():
        load_all(options, sources, landed, sems, place_of()[1])

    total = landed.shape[0]
    per_step = out_ref.shape[0]
    for i in range(per_step):
        at = position_ref[step * per_step + i]
        out_ref[i] = landed[jnp.where(at < total, at, 0)]


def collect(position, sources, place_of, steps):
    shape = sources[0][0].shape[1:]
    total = rows_of(sources)
    pairs = position.shape[0]
    flat = sum(sources, [])
    return pl.pallas_call(
        functools.partial(collect_kernel, tuple(map(len, sources)), place_of),
        grid_spec=pltpu.PrefetchScalarGridSpec(
            num_scalar_prefetch=1,
            grid=(steps,),
            in_specs=[pl.BlockSpec(memory_space=pl.ANY)] * len(flat),
            out_specs=pl.BlockSpec((pairs // steps, *shape), lambda i, _: (i, 0, 0)),
            scratch_shapes=[
                pltpu.VMEM((total, *shape), BF16),
                pltpu.SemaphoreType.DMA((len(sources),)),
            ],
        ),
        out_shape=jax.ShapeDtypeStruct((pairs, *shape), BF16),
        cost_estimate=pl.CostEstimate(
            flops=0, bytes_accessed=2 * (total + pairs) * math.prod(shape), transcendentals=0
        ),
        name="collect",
    )(position, *flat)


def project(fetched, weight_ref):
    channels = fetched.shape[-1]
    projected = jnp.dot(
        fetched, weight_ref[:, channels : 3 * channels], preferred_element_type=F32
    ).astype(BF16)
    return projected[:, :channels], projected[:, channels:]


def score(queries, keys):
    area, channels = queries.shape
    lane = lax.broadcasted_iota(jnp.int32, (area, channels), 1) // (channels // HEADS)
    zero = jnp.zeros_like(queries)
    stacked = jnp.concatenate(
        [jnp.where(lane == head, queries, zero) for head in range(HEADS)], axis=0
    )
    return lax.dot_general(
        stacked, keys, (((1,), (1,)), ((), ())), preferred_element_type=F32
    )


def blend(weights, values):
    area, channels = weights.shape[0] // HEADS, values.shape[1]
    blended = jnp.dot(weights, values, preferred_element_type=F32)
    lane = lax.broadcasted_iota(jnp.int32, (area, channels), 1) // (channels // HEADS)
    picked = blended[:area]
    for head in range(1, HEADS):
        picked = jnp.where(lane == head, blended[head * area : (head + 1) * area], picked)
    return picked


def gelu(lifted):
    inner = lifted * (0.7978845608028654 + 0.035677408136300125 * (lifted * lifted))
    return lifted * (0.5 + 0.5 * jnp.tanh(inner))


def tail_kernel(side, picks, batch, early, options, place_of, position_ref, *refs):
    late_count = sum(options)
    late = refs[:late_count]
    (
        fetched_ref,
        query_ref,
        context_ref,
        image_ref,
        qkv_ref,
        out_weight_ref,
        gain_ref,
        up_ref,
        down_ref,
        result_ref,
        landed,
        combined_ref,
        sems,
    ) = refs[late_count:]
    step = pl.program_id(0)
    last = pl.num_programs(0) - 2

    @pl.when(step == 0)
    def _():
        combined_ref[...] = jnp.zeros_like(combined_ref)
        load_all(options, late, landed, sems, place_of()[1])

    area, channels = fetched_ref.shape[1:]
    exponent = (channels // HEADS) ** (-0.5) * math.log2(math.e)
    first = jnp.minimum(step, last) * (batch * picks)

    def piece(which):
        at = position_ref[first + which]
        is_late = at >= early
        return jnp.where(is_late, landed[jnp.where(is_late, at - early, 0)], fetched_ref[which])

    previous = combined_ref[...]
    chunk = PAIR * area

    def attention(region):
        rows = pl.ds(region * area, area)
        fetched = jnp.concatenate(
            [piece(which) for which in range(region * picks, (region + 1) * picks)], axis=0
        )
        keys, values = project(fetched, qkv_ref)
        yield True
        scores = score(query_ref[rows, :], keys)
        yield True
        highest = jnp.max(scores, axis=-1, keepdims=True)
        expons = jnp.exp2((scores - highest) * exponent)
        yield True
        total = jnp.sum(expons, axis=-1, keepdims=True)
        weights = (expons * (1.0 / total)).astype(BF16)
        yield True
        attended = blend(weights, values)
        combined_ref[rows, :] = (attended + context_ref[rows, :]).astype(BF16)
        yield True

    def feed_forward(part):
        columns = pl.ds(part * PAIR * side, PAIR * side)
        image = regions_of(image_ref[:, columns, :].astype(F32), side)
        combined = previous[part * chunk : (part + 1) * chunk]
        residual = image + jnp.dot(combined, out_weight_ref[...], preferred_element_type=F32)
        yield True
        stored = residual.astype(BF16).astype(F32)
        second = normalize(stored, gain_ref[...]).astype(BF16)
        yield True
        lifted = jnp.dot(second, up_ref[...], preferred_element_type=F32)
        yield True
        hidden = gelu(lifted).astype(BF16)
        yield True
        refined = stored + jnp.dot(hidden, down_ref[...], preferred_element_type=F32)
        result_ref[:, columns, :] = strip_of(refined, side, PAIR * side).astype(BF16)
        yield True

    lines = [feed_forward(part) for part in range(batch // PAIR)]
    lines += [attention(region) for region in range(batch)]
    while lines:
        lines = [line for line in lines if next(line, None) is not None]


def tail(position, early, fetched, late, place_of, queries, context, image, weights, side, picks):
    height, width, channels = image.shape
    area = side * side
    per_row = width // side
    batch = math.gcd(per_row, 4)
    halves = per_row // batch
    steps = height // side * halves
    full = lambda a: pl.BlockSpec(a.shape, lambda i, position: (0,) * a.ndim)
    now = lambda i: jnp.minimum(i, steps - 1)
    before = lambda i: jnp.maximum(i - 1, 0)
    tokens = pl.BlockSpec((batch * area, channels), lambda i, position: (now(i), 0))
    strip = pl.BlockSpec(
        (side, batch * side, channels),
        lambda i, position: (before(i) // halves, before(i) % halves, 0),
    )
    regions = pl.BlockSpec((batch * picks, area, channels), lambda i, position: (now(i), 0, 0))
    total = rows_of(late)
    flat = sum(late, [])
    return pl.pallas_call(
        functools.partial(
            tail_kernel, side, picks, batch, early, tuple(map(len, late)), place_of
        ),
        grid_spec=pltpu.PrefetchScalarGridSpec(
            num_scalar_prefetch=1,
            grid=(steps + 1,),
            in_specs=[pl.BlockSpec(memory_space=pl.ANY)] * len(flat)
            + [regions, tokens, tokens, strip]
            + [full(w) for w in weights],
            out_specs=strip,
            scratch_shapes=[
                pltpu.VMEM((total, area, channels), BF16),
                pltpu.VMEM((batch * area, channels), BF16),
                pltpu.SemaphoreType.DMA((len(late),)),
            ],
        ),
        out_shape=jax.ShapeDtypeStruct(image.shape, BF16),
        cost_estimate=pl.CostEstimate(
            flops=image.size * 4000, bytes_accessed=16 * image.size, transcendentals=40 * image.size
        ),
        name="tail",
    )(position, *flat, fetched, queries, context, image, *weights)


def layer_blocks(block, layers):
    if layers != 4:
        return [[block]] + [
            [lax.ppermute(block, "z", [(i, i ^ step) for i in range(layers)])]
            for step in range(1, layers)
        ]

    def hop(block, pairs):
        return lax.ppermute(block, "z", pairs)

    beside = hop(block, [(0, 1), (1, 0), (2, 3), (3, 2)])
    middle = hop(block, [(1, 2), (2, 1)])
    middle_two = hop(beside, [(1, 2), (2, 1)])
    ends_two = hop(middle, [(1, 0), (2, 3)])
    ends_three = hop(middle_two, [(1, 0), (2, 3)])
    return [[block], [beside], [middle_two, ends_two], [middle, ends_three]]


def block(
    image, routes, norm_gain, qkv_weight, lce_weight, out_weight, mlp_gain, up_weight, down_weight
):
    height, _, channels = image.shape
    layers, across = lax.axis_size("z"), lax.axis_size("x")
    peers = lax.axis_size("rows") * across
    devices = peers * layers
    region_rows, region_cols, pick_count = routes.shape
    side = height // region_rows
    pair_count = region_rows * region_cols * pick_count
    capacity = max(2, 2 * pair_count // devices)
    all_cols = region_cols * layers * across

    def place_of():
        return lax.axis_index("rows") * across + lax.axis_index("x"), lax.axis_index("z")

    peer, layer = place_of()

    targets = routes.reshape(pair_count)
    target_row = targets // all_cols
    target_col = targets % all_cols
    owner_col = target_col // region_cols
    owner_layer = owner_col // across
    owner_peer = target_row // region_rows * across + owner_col % across
    local_index = target_row % region_rows * region_cols + target_col % region_cols
    owners = owner_peer * layers + owner_layer
    pairs = jnp.arange(pair_count, dtype=jnp.int32)
    earlier = (owners[:, None] == owners[None, :]) & (pairs[None, :] < pairs[:, None])
    slot = jnp.sum(earlier.astype(jnp.int32), axis=1)
    distance = owner_peer ^ peer
    step = owner_layer ^ layer
    whole, twin = (1, peers // 2), across
    lanes = -(-(layers + len(whole)) * capacity // 128) * 128
    asked = owner_peer * lanes + owner_layer * capacity + slot
    for number, far in enumerate(whole):
        through = (peer ^ twin) * lanes + (layers + number) * capacity + slot
        asked = jnp.where((step == 0) & (distance == far ^ twin), through, asked)
    slots = jnp.arange(peers * lanes, dtype=jnp.int32)
    requests = jnp.sum(
        jnp.where(asked[None, :] == slots[:, None], local_index[None, :], 0), axis=1
    )
    wanted = lax.all_to_all(
        requests.reshape(peers, 1, lanes), ("rows", "x"), 0, 0, tiled=True
    )

    margin = (lce_weight.shape[0] - 1) // 2
    normed, *edges = norm_regions(image, norm_gain, side, margin, 8)

    def swap(part, far):
        return lax.ppermute(part, ("rows", "x"), [(i, i ^ far) for i in range(peers)])

    held = layer_blocks(normed, layers)
    given = [swap(normed, far) for far in whole]
    above, below = from_sides(*edges[:2], "rows")

    tile = normed.shape[1:]
    position, total = jnp.zeros_like(slot), 0
    arrived = []

    def landing(options, *places):
        nonlocal position, total
        for condition, index in places:
            position = jnp.where(condition, total + index, position)
        total += options[0].shape[0]
        arrived[-1].append(options)

    relayed = [twin, *(far ^ twin for far in whole)]
    direct = [far for far in range(1, peers) if far not in relayed and far not in whole]
    jobs = [(0, 0, 0, twin, 0)]
    jobs += [(0, 1 + i, 1 + i, twin, layers + i) for i in range(len(whole))]
    jobs += [(1 + i, 0, 0, far, 0) for i, far in enumerate(direct)]
    jobs += [(1 + len(direct), None, 1 + len(whole), far, 1) for far in range(1, peers)]
    shapes = [(len(relayed) * capacity, *tile)] + [(capacity, *tile)] * len(direct)
    shapes += [(peers, capacity, *tile)]
    sources = [[normed], *([part] for part in given), held[1]]
    *parts, joint, low, high = pack(
        jobs, shapes, sources, place_of, wanted, capacity, layers, (above, below, *edges[2:])
    )
    got = [swap(part, far) for part, far in zip(parts, [twin, *direct])]
    joint = lax.all_to_all(joint, ("rows", "x"), 0, 0, tiled=True)
    around = (above, below, *from_sides(low, high, ("z", "x")))
    arrived.append([])
    landing([normed], ((step == 0) & (distance == 0), local_index))
    for far, part in zip(whole, given):
        landing([part], ((step == 0) & (distance == far), local_index))
    landing(
        [got[0]],
        *(
            ((step == 0) & (distance == far), i * capacity + slot)
            for i, far in enumerate(relayed)
        ),
    )
    for far, part in zip(direct, got[1:]):
        landing([part], ((step == 0) & (distance == far), slot))
    landing(held[1], ((step == 1) & (distance == 0), local_index))
    landing(
        [joint.reshape(-1, *tile)],
        ((step == 1) & (distance != 0), owner_peer * capacity + slot),
    )

    for chunk in range(2, layers):
        last = chunk == layers - 1
        jobs = [(0 if last else far - 1, None if last else 0, 0, far, chunk) for far in range(1, peers)]
        shapes = [(peers, capacity, *tile)] if last else [(capacity, *tile)] * (peers - 1)
        parts = pack(jobs, shapes, [held[chunk]], place_of, wanted, capacity, layers)
        if last:
            got = lax.all_to_all(parts[0], ("rows", "x"), 0, 0, tiled=True)
        else:
            got = [swap(part, far) for far, part in enumerate(parts, 1)]
        early = total
        arrived.append([])
        landing(held[chunk], ((step == chunk) & (distance == 0), local_index))
        if last:
            elsewhere = (step == chunk) & (distance != 0)
            landing([got.reshape(-1, *tile)], (elsewhere, owner_peer * capacity + slot))
        else:
            for far, part in enumerate(got, 1):
                landing([part], ((step == chunk) & (distance == far), slot))
    late = arrived.pop()
    fetched = collect(position, sum(arrived, []), place_of, math.gcd(pair_count, 8))

    context, queries = context_and_queries(
        image, around, norm_gain, qkv_weight, lce_weight, side, margin
    )
    weights = (
        qkv_weight,
        out_weight,
        mlp_gain.reshape(1, channels),
        up_weight,
        down_weight,
    )
    return tail(position, early, fetched, late, place_of, queries, context, image, weights, side, pick_count)


def solution(mesh):
    devices = mesh.devices
    layers = len({device.coords[2] for device in devices[0]})
    split = Mesh(
        devices.reshape(devices.shape[0], layers, devices.shape[1] // layers), ("rows", "z", "x")
    )
    grid = P("rows", ("z", "x"), None)
    in_specs = (grid, grid, P(), P(), P(), P(), P(), P(), P())
    return jax.shard_map(block, mesh=split, in_specs=in_specs, out_specs=grid, check_vma=False)
```

```python
import functools
import math

import jax
import jax.numpy as jnp
from jax import lax
from jax.experimental import pallas as pl
from jax.experimental.pallas import tpu as pltpu
from jax.sharding import Mesh
from jax.sharding import PartitionSpec as P

HEADS = 4
PAIR = 2
EPSILON = 1e-06
F32 = jnp.float32
BF16 = jnp.bfloat16


def with_pairs(parts, axis, count):
    links = ([], [])
    for i in range(count - 1):
        links[i % 2].extend([(i, i + 1), (i + 1, i)])
    return [lax.ppermute(part, axis, pairs) for part, pairs in zip(parts, links)]


def either(flag, yes, no):
    return jnp.where(flag, yes, no)


def normalize(floats, gain):
    centered = floats - jnp.mean(floats, axis=-1, keepdims=True)
    spread = jnp.mean(centered * centered, axis=-1, keepdims=True)
    return centered * lax.rsqrt(spread + EPSILON) * gain


def regions_of(strip, side):
    height, width, channels = strip.shape
    return (
        strip.reshape(height, width // side, side, channels)
        .transpose(1, 0, 2, 3)
        .reshape(height * width, channels)
    )


def strip_of(tokens, side, width):
    channels = tokens.shape[-1]
    return (
        tokens.reshape(width // side, side, side, channels)
        .transpose(1, 0, 2, 3)
        .reshape(side, width, channels)
    )


def norm_kernel(side, evens_of, image_ref, gain_ref, out_ref, *edge_refs):
    step = pl.program_id(0)
    *row_refs, left_ref, right_ref = edge_refs
    tokens = image_ref[...]
    normed = normalize(tokens.astype(F32), gain_ref[...])
    out_ref[...] = regions_of(normed, side).astype(BF16).reshape(out_ref.shape)
    margin, width, border = row_refs[0].shape[0], tokens.shape[1], left_ref.shape[1]
    left_ref[...] = image_ref[:, pl.ds(0, border), :]
    right_ref[...] = image_ref[:, pl.ds(width - border, border), :]
    row_even = evens_of()[0]

    def put(even, odd, first):
        def store(ref):
            ref[...] = image_ref[pl.ds(first, margin)]

        pl.when(row_even)(lambda: store(row_refs[even]))
        pl.when(~row_even)(lambda: store(row_refs[odd]))

    pl.when(step == 0)(lambda: put(1, 0, 0))
    pl.when(step == pl.num_programs(0) - 1)(lambda: put(0, 1, side - margin))


def norm_regions(image, gain, side, margin, border, evens_of):
    height, width, channels = image.shape
    per_row = width // side
    edge = jax.ShapeDtypeStruct((margin, width, channels), BF16)
    flank = jax.ShapeDtypeStruct((height, border, channels), BF16)
    return pl.pallas_call(
        functools.partial(norm_kernel, side, evens_of),
        grid=(height // side,),
        in_specs=[
            pl.BlockSpec((side, width, channels), lambda i: (i, 0, 0)),
            pl.BlockSpec((1, channels), lambda i: (0, 0)),
        ],
        out_specs=[
            pl.BlockSpec((per_row, side * side, channels), lambda i: (i, 0, 0)),
            pl.BlockSpec(edge.shape, lambda i: (0, 0, 0)),
            pl.BlockSpec(edge.shape, lambda i: (0, 0, 0)),
            pl.BlockSpec((side, border, channels), lambda i: (i, 0, 0)),
            pl.BlockSpec((side, border, channels), lambda i: (i, 0, 0)),
        ],
        out_shape=[
            jax.ShapeDtypeStruct((height // side * per_row, side * side, channels), BF16),
            edge,
            edge,
            flank,
            flank,
        ],
        cost_estimate=pl.CostEstimate(
            flops=10 * image.size, bytes_accessed=4 * image.size, transcendentals=0
        ),
        name="norm_regions",
    )(image, gain.reshape(1, channels))


def context_kernel(
    side,
    margin,
    evens_of,
    image_ref,
    row_pair_ref,
    row_other_ref,
    col_pair_ref,
    col_other_ref,
    gain_ref,
    weight_ref,
    lce_ref,
    context_ref,
    query_ref,
    padded,
):
    step = pl.program_id(0)
    height, width, channels = image_ref.shape
    border = col_pair_ref.shape[1]

    @pl.when(step == 0)
    def _():
        row_even, col_even = evens_of()
        inner = pl.ds(border, width)
        paired, other = row_pair_ref[...].astype(F32), row_other_ref[...].astype(F32)
        padded[:margin, inner] = either(row_even, other, paired)
        padded[pl.ds(margin, height), inner] = image_ref[...].astype(F32)
        padded[pl.ds(margin + height, margin), inner] = either(row_even, paired, other)
        paired, other = col_pair_ref[...].astype(F32), col_other_ref[...].astype(F32)
        padded[:, :border] = either(col_even, other, paired)
        padded[:, pl.ds(border + width, border)] = either(col_even, paired, other)

    rows = side + 2 * margin
    strip = padded[pl.ds(step * side, rows)]
    wide = strip.shape[1]
    normed = normalize(strip, gain_ref[...]).astype(BF16).reshape(rows * wide, channels)
    weight = jnp.concatenate([weight_ref[:, :channels], weight_ref[:, 2 * channels :]], axis=1)
    projected = jnp.dot(normed, weight, preferred_element_type=F32).astype(BF16)
    values = projected[:, channels:].astype(F32).reshape(rows, wide, channels)
    summed = jnp.zeros((side, width, channels), F32)
    for col in range(2 * margin + 1):
        moved = pltpu.roll(values, wide - (border - margin + col), 1)[:, :width]
        for row in range(2 * margin + 1):
            summed = summed + moved[row : row + side] * lce_ref[row, pl.ds(col, 1), :]
    context_ref[...] = regions_of(summed, side)
    queries = projected[:, :channels].astype(F32).reshape(rows, wide, channels)
    inner = queries[margin : margin + side, border : border + width]
    query_ref[...] = regions_of(inner, side).astype(BF16)


def context_and_queries(image, around, gain, qkv_weight, lce_weight, side, margin, evens_of):
    height, width, channels = image.shape
    border = around[-1].shape[1]
    tokens = height * width
    full = lambda a: pl.BlockSpec(a.shape, lambda i: (0,) * a.ndim)
    operands = (image, *around, gain.reshape(1, channels), qkv_weight, lce_weight)
    return pl.pallas_call(
        functools.partial(context_kernel, side, margin, evens_of),
        grid=(height // side,),
        in_specs=[full(a) for a in operands],
        out_specs=[
            pl.BlockSpec((side * width, channels), lambda i: (i, 0)),
            pl.BlockSpec((side * width, channels), lambda i: (i, 0)),
        ],
        out_shape=[
            jax.ShapeDtypeStruct((tokens, channels), F32),
            jax.ShapeDtypeStruct((tokens, channels), BF16),
        ],
        scratch_shapes=[
            pltpu.VMEM((height + 2 * margin, width + 2 * border, channels), F32),
        ],
        cost_estimate=pl.CostEstimate(
            flops=tokens * channels * 600, bytes_accessed=10 * tokens * channels, transcendentals=0
        ),
        name="context",
    )(*operands)


def is_inside(layer):
    return (layer == 1) | (layer == 2)


def frame_kernel(evens, row_refs, flank_refs, out_refs):
    row_even, col_even = evens
    margin, width = row_refs[0].shape[:2]
    height, border = flank_refs[0].shape[:2]
    paired, other = row_refs[0][...], row_refs[1][...]
    above, below = either(row_even, other, paired), either(row_even, paired, other)
    for out_ref, flag in ((out_refs[0], col_even), (out_refs[1], ~col_even)):
        right = lambda rows: rows[:, width - border :]
        left = lambda rows: rows[:, :border]
        out_ref[pl.ds(0, margin)] = either(flag, right(above), left(above))
        out_ref[pl.ds(margin, height)] = either(flag, flank_refs[1][...], flank_refs[0][...])
        out_ref[pl.ds(margin + height, margin)] = either(flag, right(below), left(below))


def pack_kernel(jobs, options, outputs, evens_of, capacity, layers, place_of, wanted_ref, *refs):
    peer, layer = place_of()
    sources = refs[: sum(options)]
    outs = refs[len(refs) - outputs :]
    if evens_of is not None:
        edges = refs[sum(options) : sum(options) + 4]
        frame_kernel(evens_of(), edges[:2], edges[2:], outs[-2:])
    inside = is_inside(layer)

    def fill(source_ref, out_ref, place, distance, column):
        other = peer ^ distance
        base = ((layer ^ column) if column < layers else column) * capacity
        for slot in range(capacity):
            region = source_ref[wanted_ref[other, 0, base + slot]]
            if place is None:
                out_ref[other, slot] = region
            else:
                out_ref[place * capacity + slot] = region

    def fill_all(shift, chosen):
        for out, place, source, distance, column in chosen:
            at = sum(options[:source]) + shift
            fill(sources[at], outs[out], place, distance, column)

    fill_all(0, [job for job in jobs if options[job[2]] == 1])
    paired = [job for job in jobs if options[job[2]] == 2]
    if paired:
        pl.when(inside)(functools.partial(fill_all, 0, paired))
        pl.when(~inside)(functools.partial(fill_all, 1, paired))


def pack(jobs, shapes, sources, place_of, wanted, capacity, layers, frame=(), evens_of=None):
    flat = sum(sources, [])
    if frame:
        margin, (height, border, channels) = frame[0].shape[0], frame[2].shape
        shapes = shapes + [(height + 2 * margin, border, channels)] * 2
    in_vmem = pl.BlockSpec(memory_space=pltpu.VMEM)
    return pl.pallas_call(
        functools.partial(
            pack_kernel,
            tuple(jobs),
            tuple(map(len, sources)),
            len(shapes),
            evens_of,
            capacity,
            layers,
            place_of,
        ),
        in_specs=[pl.BlockSpec(memory_space=pltpu.SMEM)] + [in_vmem] * (len(flat) + len(frame)),
        out_specs=[in_vmem] * len(shapes),
        out_shape=[jax.ShapeDtypeStruct(a, BF16) for a in shapes],
        cost_estimate=pl.CostEstimate(
            flops=0, bytes_accessed=4 * sum(map(math.prod, shapes)), transcendentals=0
        ),
        name="pack",
    )(wanted, *flat, *frame)


def load_all(options, sources, landed, sems, layer):
    waits, start, at = [], 0, 0
    inside = is_inside(layer)
    for i, count in enumerate(options):
        size = sources[at].shape[0]
        copies = [
            pltpu.make_async_copy(source, landed.at[pl.ds(start, size)], sems.at[i])
            for source in sources[at : at + count]
        ]
        if count == 1:
            copies[0].start()
        else:
            pl.when(inside)(copies[0].start)
            pl.when(~inside)(copies[1].start)
        waits.append(copies[0])
        start += size
        at += count
    for copy in waits:
        copy.wait()


def rows_of(sources):
    return sum(options[0].shape[0] for options in sources)


def collect_kernel(options, place_of, position_ref, *refs):
    sources, out_ref, landed, sems = refs[: sum(options)], refs[-3], refs[-2], refs[-1]
    step = pl.program_id(0)

    @pl.when(step == 0)
    def _():
        load_all(options, sources, landed, sems, place_of()[1])

    total = landed.shape[0]
    per_step = out_ref.shape[0]
    for i in range(per_step):
        at = position_ref[step * per_step + i]
        out_ref[i] = landed[jnp.where(at < total, at, 0)]


def collect(position, sources, place_of, steps):
    shape = sources[0][0].shape[1:]
    total = rows_of(sources)
    pairs = position.shape[0]
    flat = sum(sources, [])
    return pl.pallas_call(
        functools.partial(collect_kernel, tuple(map(len, sources)), place_of),
        grid_spec=pltpu.PrefetchScalarGridSpec(
            num_scalar_prefetch=1,
            grid=(steps,),
            in_specs=[pl.BlockSpec(memory_space=pl.ANY)] * len(flat),
            out_specs=pl.BlockSpec((pairs // steps, *shape), lambda i, _: (i, 0, 0)),
            scratch_shapes=[
                pltpu.VMEM((total, *shape), BF16),
                pltpu.SemaphoreType.DMA((len(sources),)),
            ],
        ),
        out_shape=jax.ShapeDtypeStruct((pairs, *shape), BF16),
        cost_estimate=pl.CostEstimate(
            flops=0, bytes_accessed=2 * (total + pairs) * math.prod(shape), transcendentals=0
        ),
        name="collect",
    )(position, *flat)


def project(fetched, weight_ref):
    channels = fetched.shape[-1]
    projected = jnp.dot(
        fetched, weight_ref[:, channels : 3 * channels], preferred_element_type=F32
    ).astype(BF16)
    return projected[:, :channels], projected[:, channels:]


def score(queries, keys):
    area, channels = queries.shape
    lane = lax.broadcasted_iota(jnp.int32, (area, channels), 1) // (channels // HEADS)
    zero = jnp.zeros_like(queries)
    stacked = jnp.concatenate(
        [jnp.where(lane == head, queries, zero) for head in range(HEADS)], axis=0
    )
    return lax.dot_general(
        stacked, keys, (((1,), (1,)), ((), ())), preferred_element_type=F32
    )


def blend(weights, values):
    area, channels = weights.shape[0] // HEADS, values.shape[1]
    blended = jnp.dot(weights, values, preferred_element_type=F32)
    lane = lax.broadcasted_iota(jnp.int32, (area, channels), 1) // (channels // HEADS)
    picked = blended[:area]
    for head in range(1, HEADS):
        picked = jnp.where(lane == head, blended[head * area : (head + 1) * area], picked)
    return picked


def gelu(lifted):
    inner = lifted * (0.7978845608028654 + 0.035677408136300125 * (lifted * lifted))
    return lifted * (0.5 + 0.5 * jnp.tanh(inner))


def tail_kernel(
    side,
    picks,
    batch,
    early,
    position_ref,
    late_ref,
    fetched_ref,
    query_ref,
    context_ref,
    image_ref,
    qkv_ref,
    out_weight_ref,
    gain_ref,
    up_ref,
    down_ref,
    result_ref,
    combined_ref,
):
    step = pl.program_id(0)
    last = pl.num_programs(0) - 2

    area, channels = fetched_ref.shape[1:]
    exponent = (channels // HEADS) ** (-0.5) * math.log2(math.e)
    first = jnp.minimum(step, last) * (batch * picks)

    def piece(which):
        at = position_ref[first + which]
        is_late = at >= early
        return jnp.where(is_late, late_ref[jnp.where(is_late, at - early, 0)], fetched_ref[which])

    chunk = PAIR * area

    def attention(region):
        rows = pl.ds(region * area, area)
        fetched = jnp.concatenate(
            [piece(which) for which in range(region * picks, (region + 1) * picks)], axis=0
        )
        keys, values = project(fetched, qkv_ref)
        yield True
        scores = score(query_ref[rows, :], keys)
        yield True
        highest = jnp.max(scores, axis=-1, keepdims=True)
        expons = jnp.exp2((scores - highest) * exponent)
        yield True
        total = jnp.sum(expons, axis=-1, keepdims=True)
        weights = (expons * (1.0 / total)).astype(BF16)
        yield True
        attended = blend(weights, values)
        combined_ref[rows, :] = (attended + context_ref[rows, :]).astype(BF16)
        yield True

    def feed_forward(part):
        columns = pl.ds(part * PAIR * side, PAIR * side)
        image = regions_of(image_ref[:, columns, :].astype(F32), side)
        combined = combined_ref[pl.ds(part * chunk, chunk), :]
        residual = image + jnp.dot(combined, out_weight_ref[...], preferred_element_type=F32)
        yield True
        stored = residual.astype(BF16).astype(F32)
        second = normalize(stored, gain_ref[...]).astype(BF16)
        yield True
        lifted = jnp.dot(second, up_ref[...], preferred_element_type=F32)
        yield True
        hidden = gelu(lifted).astype(BF16)
        yield True
        refined = stored + jnp.dot(hidden, down_ref[...], preferred_element_type=F32)
        result_ref[:, columns, :] = strip_of(refined, side, PAIR * side).astype(BF16)
        yield True

    def run(forward, attend):
        lines = [feed_forward(part) for part in range(batch // PAIR)] if forward else []
        lines += [attention(region) for region in range(batch)] if attend else []
        while lines:
            lines = [line for line in lines if next(line, None) is not None]

    pl.when(step == 0)(lambda: run(False, True))
    pl.when((step > 0) & (step <= last))(lambda: run(True, True))
    pl.when(step > last)(lambda: run(True, False))


def tail(position, early, fetched, late, queries, context, image, weights, side, picks):
    height, width, channels = image.shape
    area = side * side
    per_row = width // side
    batch = math.gcd(per_row, 4)
    halves = per_row // batch
    steps = height // side * halves
    full = lambda a: pl.BlockSpec(a.shape, lambda i, position: (0,) * a.ndim)
    now = lambda i: jnp.minimum(i, steps - 1)
    before = lambda i: jnp.maximum(i - 1, 0)
    tokens = pl.BlockSpec((batch * area, channels), lambda i, position: (now(i), 0))
    strip = pl.BlockSpec(
        (side, batch * side, channels),
        lambda i, position: (before(i) // halves, before(i) % halves, 0),
    )
    regions = pl.BlockSpec((batch * picks, area, channels), lambda i, position: (now(i), 0, 0))
    return pl.pallas_call(
        functools.partial(tail_kernel, side, picks, batch, early),
        grid_spec=pltpu.PrefetchScalarGridSpec(
            num_scalar_prefetch=1,
            grid=(steps + 1,),
            in_specs=[pl.BlockSpec(memory_space=pltpu.VMEM), regions, tokens, tokens, strip]
            + [full(w) for w in weights],
            out_specs=strip,
            scratch_shapes=[pltpu.VMEM((batch * area, channels), BF16)],
        ),
        out_shape=jax.ShapeDtypeStruct(image.shape, BF16),
        cost_estimate=pl.CostEstimate(
            flops=image.size * 4000, bytes_accessed=16 * image.size, transcendentals=40 * image.size
        ),
        name="tail",
    )(position, late, fetched, queries, context, image, *weights)


def layer_blocks(block, layers):
    if layers != 4:
        return [[block]] + [
            [lax.ppermute(block, "z", [(i, i ^ step) for i in range(layers)])]
            for step in range(1, layers)
        ]

    def hop(block, pairs):
        return lax.ppermute(block, "z", pairs)

    beside = hop(block, [(0, 1), (1, 0), (2, 3), (3, 2)])
    middle = hop(block, [(1, 2), (2, 1)])
    middle_two = hop(beside, [(1, 2), (2, 1)])
    ends_two = hop(middle, [(1, 0), (2, 3)])
    ends_three = hop(middle_two, [(1, 0), (2, 3)])
    return [[block], [beside], [middle_two, ends_two], [middle, ends_three]]


def block(
    image, routes, norm_gain, qkv_weight, lce_weight, out_weight, mlp_gain, up_weight, down_weight
):
    height, _, channels = image.shape
    layers, across = lax.axis_size("z"), lax.axis_size("x")
    peers = lax.axis_size("rows") * across
    devices = peers * layers
    region_rows, region_cols, pick_count = routes.shape
    side = height // region_rows
    pair_count = region_rows * region_cols * pick_count
    capacity = max(2, 2 * pair_count // devices)
    all_cols = region_cols * layers * across

    def place_of():
        return lax.axis_index("rows") * across + lax.axis_index("x"), lax.axis_index("z")

    def evens_of():
        return lax.axis_index("rows") % 2 == 0, lax.axis_index("x") % 2 == 0

    peer, layer = place_of()

    targets = routes.reshape(pair_count)
    target_row = targets // all_cols
    target_col = targets % all_cols
    owner_col = target_col // region_cols
    owner_layer = owner_col // across
    owner_peer = target_row // region_rows * across + owner_col % across
    local_index = target_row % region_rows * region_cols + target_col % region_cols
    owners = owner_peer * layers + owner_layer
    pairs = jnp.arange(pair_count, dtype=jnp.int32)
    earlier = (owners[:, None] == owners[None, :]) & (pairs[None, :] < pairs[:, None])
    slot = jnp.sum(earlier.astype(jnp.int32), axis=1)
    distance = owner_peer ^ peer
    step = owner_layer ^ layer
    whole, twin = (1, peers // 2), across
    lanes = -(-(layers + len(whole)) * capacity // 128) * 128
    asked = owner_peer * lanes + owner_layer * capacity + slot
    for number, far in enumerate(whole):
        through = (peer ^ twin) * lanes + (layers + number) * capacity + slot
        asked = jnp.where((step == 0) & (distance == far ^ twin), through, asked)
    slots = jnp.arange(peers * lanes, dtype=jnp.int32)
    requests = jnp.sum(
        jnp.where(asked[None, :] == slots[:, None], local_index[None, :], 0), axis=1
    )
    wanted = lax.all_to_all(
        requests.reshape(peers, 1, lanes), ("rows", "x"), 0, 0, tiled=True
    )

    margin = (lce_weight.shape[0] - 1) // 2
    normed, *edges = norm_regions(image, norm_gain, side, margin, 8, evens_of)

    def swap(part, far):
        return lax.ppermute(part, ("rows", "x"), [(i, i ^ far) for i in range(peers)])

    held = layer_blocks(normed, layers)
    given = [swap(normed, far) for far in whole]
    near_rows = with_pairs(edges[:2], "rows", lax.axis_size("rows"))

    tile = normed.shape[1:]
    position, total = jnp.zeros_like(slot), 0
    arrived = []

    def landing(options, *places):
        nonlocal position, total
        for condition, index in places:
            position = jnp.where(condition, total + index, position)
        total += options[0].shape[0]
        arrived[-1].append(options)

    relayed = [twin, *(far ^ twin for far in whole)]
    direct = [far for far in range(1, peers) if far not in relayed and far not in whole]
    jobs = [(0, 0, 0, twin, 0)]
    jobs += [(0, 1 + i, 1 + i, twin, layers + i) for i in range(len(whole))]
    jobs += [(1 + i, 0, 0, far, 0) for i, far in enumerate(direct)]
    jobs += [(1 + len(direct), None, 1 + len(whole), far, 1) for far in range(1, peers)]
    shapes = [(len(relayed) * capacity, *tile)] + [(capacity, *tile)] * len(direct)
    shapes += [(peers, capacity, *tile)]
    sources = [[normed], *([part] for part in given), held[1]]
    *parts, joint, paired, other = pack(
        jobs,
        shapes,
        sources,
        place_of,
        wanted,
        capacity,
        layers,
        (*near_rows, *edges[2:]),
        evens_of,
    )
    got = [swap(part, far) for part, far in zip(parts, [twin, *direct])]
    joint = lax.all_to_all(joint, ("rows", "x"), 0, 0, tiled=True)
    around = (*near_rows, *with_pairs((paired, other), ("z", "x"), layers * across))
    arrived.append([])
    landing([normed], ((step == 0) & (distance == 0), local_index))
    for far, part in zip(whole, given):
        landing([part], ((step == 0) & (distance == far), local_index))
    landing(
        [got[0]],
        *(
            ((step == 0) & (distance == far), i * capacity + slot)
            for i, far in enumerate(relayed)
        ),
    )
    for far, part in zip(direct, got[1:]):
        landing([part], ((step == 0) & (distance == far), slot))
    landing(held[1], ((step == 1) & (distance == 0), local_index))
    landing(
        [joint.reshape(-1, *tile)],
        ((step == 1) & (distance != 0), owner_peer * capacity + slot),
    )

    for chunk in range(2, layers):
        last = chunk == layers - 1
        jobs = [(0 if last else far - 1, None if last else 0, 0, far, chunk) for far in range(1, peers)]
        shapes = [(peers, capacity, *tile)] if last else [(capacity, *tile)] * (peers - 1)
        parts = pack(jobs, shapes, [held[chunk]], place_of, wanted, capacity, layers)
        if last:
            got = lax.all_to_all(parts[0], ("rows", "x"), 0, 0, tiled=True)
        else:
            got = [swap(part, far) for far, part in enumerate(parts, 1)]
        landing(held[chunk], ((step == chunk) & (distance == 0), local_index))
        if last:
            early = total
            arrived.append([])
            elsewhere = (step == chunk) & (distance != 0)
            landing([got.reshape(-1, *tile)], (elsewhere, owner_peer * capacity + slot))
        else:
            for far, part in enumerate(got, 1):
                landing([part], ((step == chunk) & (distance == far), slot))
    ((late,),) = arrived.pop()
    fetched = collect(position, sum(arrived, []), place_of, math.gcd(pair_count, 8))

    context, queries = context_and_queries(
        image, around, norm_gain, qkv_weight, lce_weight, side, margin, evens_of
    )
    weights = (
        qkv_weight,
        out_weight,
        mlp_gain.reshape(1, channels),
        up_weight,
        down_weight,
    )
    return tail(position, early, fetched, late, queries, context, image, weights, side, pick_count)


def solution(mesh):
    devices = mesh.devices
    layers = len({device.coords[2] for device in devices[0]})
    split = Mesh(
        devices.reshape(devices.shape[0], layers, devices.shape[1] // layers), ("rows", "z", "x")
    )
    grid = P("rows", ("z", "x"), None)
    in_specs = (grid, grid, P(), P(), P(), P(), P(), P(), P())
    return jax.shard_map(block, mesh=split, in_specs=in_specs, out_specs=grid, check_vma=False)
```

```python
import functools
import math

import jax
import jax.numpy as jnp
from jax import lax
from jax.experimental import pallas as pl
from jax.experimental.pallas import tpu as pltpu
from jax.sharding import Mesh
from jax.sharding import PartitionSpec as P

HEADS = 4
PAIR = 2
EPSILON = 1e-06
F32 = jnp.float32
BF16 = jnp.bfloat16


def with_pairs(parts, axis, count):
    links = ([], [])
    for i in range(count - 1):
        links[i % 2].extend([(i, i + 1), (i + 1, i)])
    return [lax.ppermute(part, axis, pairs) for part, pairs in zip(parts, links)]


def either(flag, yes, no):
    return jnp.where(flag, yes, no)


def normalize(floats, gain):
    centered = floats - jnp.mean(floats, axis=-1, keepdims=True)
    spread = jnp.mean(centered * centered, axis=-1, keepdims=True)
    return centered * lax.rsqrt(spread + EPSILON) * gain


def regions_of(strip, side):
    height, width, channels = strip.shape
    return (
        strip.reshape(height, width // side, side, channels)
        .transpose(1, 0, 2, 3)
        .reshape(height * width, channels)
    )


def strip_of(tokens, side, width):
    channels = tokens.shape[-1]
    return (
        tokens.reshape(width // side, side, side, channels)
        .transpose(1, 0, 2, 3)
        .reshape(side, width, channels)
    )


def norm_kernel(side, evens_of, image_ref, gain_ref, out_ref, *edge_refs):
    step = pl.program_id(0)
    *row_refs, left_ref, right_ref = edge_refs
    tokens = image_ref[...]
    normed = normalize(tokens.astype(F32), gain_ref[...])
    out_ref[...] = regions_of(normed, side).astype(BF16).reshape(out_ref.shape)
    margin, width, border = row_refs[0].shape[0], tokens.shape[1], left_ref.shape[1]
    left_ref[...] = image_ref[:, pl.ds(0, border), :]
    right_ref[...] = image_ref[:, pl.ds(width - border, border), :]
    row_even = evens_of()[0]

    def put(even, odd, first):
        def store(ref):
            ref[...] = image_ref[pl.ds(first, margin)]

        pl.when(row_even)(lambda: store(row_refs[even]))
        pl.when(~row_even)(lambda: store(row_refs[odd]))

    pl.when(step == 0)(lambda: put(1, 0, 0))
    pl.when(step == pl.num_programs(0) - 1)(lambda: put(0, 1, side - margin))


def norm_regions(image, gain, side, margin, border, evens_of):
    height, width, channels = image.shape
    per_row = width // side
    edge = jax.ShapeDtypeStruct((margin, width, channels), BF16)
    flank = jax.ShapeDtypeStruct((height, border, channels), BF16)
    return pl.pallas_call(
        functools.partial(norm_kernel, side, evens_of),
        grid=(height // side,),
        in_specs=[
            pl.BlockSpec((side, width, channels), lambda i: (i, 0, 0)),
            pl.BlockSpec((1, channels), lambda i: (0, 0)),
        ],
        out_specs=[
            pl.BlockSpec((per_row, side * side, channels), lambda i: (i, 0, 0)),
            pl.BlockSpec(edge.shape, lambda i: (0, 0, 0)),
            pl.BlockSpec(edge.shape, lambda i: (0, 0, 0)),
            pl.BlockSpec((side, border, channels), lambda i: (i, 0, 0)),
            pl.BlockSpec((side, border, channels), lambda i: (i, 0, 0)),
        ],
        out_shape=[
            jax.ShapeDtypeStruct((height // side * per_row, side * side, channels), BF16),
            edge,
            edge,
            flank,
            flank,
        ],
        cost_estimate=pl.CostEstimate(
            flops=10 * image.size, bytes_accessed=4 * image.size, transcendentals=0
        ),
        name="norm_regions",
    )(image, gain.reshape(1, channels))


def is_inside(layer):
    return (layer == 1) | (layer == 2)


def frame_kernel(evens, row_refs, flank_refs, out_refs):
    row_even, col_even = evens
    margin, width = row_refs[0].shape[:2]
    height, border = flank_refs[0].shape[:2]
    paired, other = row_refs[0][...], row_refs[1][...]
    above, below = either(row_even, other, paired), either(row_even, paired, other)
    for out_ref, flag in ((out_refs[0], col_even), (out_refs[1], ~col_even)):
        right = lambda rows: rows[:, width - border :]
        left = lambda rows: rows[:, :border]
        out_ref[pl.ds(0, margin)] = either(flag, right(above), left(above))
        out_ref[pl.ds(margin, height)] = either(flag, flank_refs[1][...], flank_refs[0][...])
        out_ref[pl.ds(margin + height, margin)] = either(flag, right(below), left(below))


def pack_kernel(jobs, options, outputs, evens_of, capacity, layers, place_of, wanted_ref, *refs):
    peer, layer = place_of()
    sources = refs[: sum(options)]
    outs = refs[len(refs) - outputs :]
    if evens_of is not None:
        edges = refs[sum(options) : sum(options) + 4]
        frame_kernel(evens_of(), edges[:2], edges[2:], outs[-2:])
    inside = is_inside(layer)

    def fill(source_ref, out_ref, place, distance, column):
        other = peer ^ distance
        base = ((layer ^ column) if column < layers else column) * capacity
        for slot in range(capacity):
            region = source_ref[wanted_ref[other, 0, base + slot]]
            if place is None:
                out_ref[other, slot] = region
            else:
                out_ref[place * capacity + slot] = region

    def fill_all(shift, chosen):
        for out, place, source, distance, column in chosen:
            at = sum(options[:source]) + shift
            fill(sources[at], outs[out], place, distance, column)

    fill_all(0, [job for job in jobs if options[job[2]] == 1])
    paired = [job for job in jobs if options[job[2]] == 2]
    if paired:
        pl.when(inside)(functools.partial(fill_all, 0, paired))
        pl.when(~inside)(functools.partial(fill_all, 1, paired))


def pack(jobs, shapes, sources, place_of, wanted, capacity, layers, frame=(), evens_of=None):
    flat = sum(sources, [])
    if frame:
        margin, (height, border, channels) = frame[0].shape[0], frame[2].shape
        shapes = shapes + [(height + 2 * margin, border, channels)] * 2
    in_vmem = pl.BlockSpec(memory_space=pltpu.VMEM)
    return pl.pallas_call(
        functools.partial(
            pack_kernel,
            tuple(jobs),
            tuple(map(len, sources)),
            len(shapes),
            evens_of,
            capacity,
            layers,
            place_of,
        ),
        in_specs=[pl.BlockSpec(memory_space=pltpu.SMEM)] + [in_vmem] * (len(flat) + len(frame)),
        out_specs=[in_vmem] * len(shapes),
        out_shape=[jax.ShapeDtypeStruct(a, BF16) for a in shapes],
        cost_estimate=pl.CostEstimate(
            flops=0, bytes_accessed=4 * sum(map(math.prod, shapes)), transcendentals=0
        ),
        name="pack",
    )(wanted, *flat, *frame)


def load_all(options, sources, landed, sems, layer, wait):
    start, at = 0, 0
    inside = is_inside(layer)
    for i, count in enumerate(options):
        size = sources[at].shape[0]
        copies = [
            pltpu.make_async_copy(source, landed.at[pl.ds(start, size)], sems.at[i])
            for source in sources[at : at + count]
        ]
        if wait:
            copies[0].wait()
        elif count == 1:
            copies[0].start()
        else:
            pl.when(inside)(copies[0].start)
            pl.when(~inside)(copies[1].start)
        start += size
        at += count


def rows_of(sources):
    return sum(options[0].shape[0] for options in sources)


def context_kernel(
    side,
    margin,
    evens_of,
    place_of,
    options,
    position_ref,
    image_ref,
    row_pair_ref,
    row_other_ref,
    col_pair_ref,
    col_other_ref,
    gain_ref,
    weight_ref,
    lce_ref,
    *refs,
):
    sources = refs[: sum(options)]
    context_ref, query_ref, fetched_ref, padded, landed, sems = refs[sum(options) :]
    step = pl.program_id(0)
    height, width, channels = image_ref.shape
    strips = height // side
    border = col_pair_ref.shape[1]

    @pl.when(step == 0)
    def _():
        load_all(options, sources, landed, sems, place_of()[1], False)
        row_even, col_even = evens_of()
        inner = pl.ds(border, width)
        paired, other = row_pair_ref[...].astype(F32), row_other_ref[...].astype(F32)
        padded[:margin, inner] = either(row_even, other, paired)
        padded[pl.ds(margin, height), inner] = image_ref[...].astype(F32)
        padded[pl.ds(margin + height, margin), inner] = either(row_even, paired, other)
        paired, other = col_pair_ref[...].astype(F32), col_other_ref[...].astype(F32)
        padded[:, :border] = either(col_even, other, paired)
        padded[:, pl.ds(border + width, border)] = either(col_even, paired, other)

    @pl.when(step < strips)
    def _():
        rows = side + 2 * margin
        strip = padded[pl.ds(jnp.minimum(step, strips - 1) * side, rows)]
        wide = strip.shape[1]
        normed = normalize(strip, gain_ref[...]).astype(BF16).reshape(rows * wide, channels)
        weight = jnp.concatenate([weight_ref[:, :channels], weight_ref[:, 2 * channels :]], axis=1)
        projected = jnp.dot(normed, weight, preferred_element_type=F32).astype(BF16)
        values = projected[:, channels:].astype(F32).reshape(rows, wide, channels)
        summed = jnp.zeros((side, width, channels), F32)
        for col in range(2 * margin + 1):
            moved = pltpu.roll(values, wide - (border - margin + col), 1)[:, :width]
            for row in range(2 * margin + 1):
                summed = summed + moved[row : row + side] * lce_ref[row, pl.ds(col, 1), :]
        context_ref[...] = regions_of(summed, side)
        queries = projected[:, :channels].astype(F32).reshape(rows, wide, channels)
        inner = queries[margin : margin + side, border : border + width]
        query_ref[...] = regions_of(inner, side).astype(BF16)

    @pl.when(step == strips)
    def _():
        load_all(options, sources, landed, sems, place_of()[1], True)

    @pl.when(step >= strips)
    def _():
        total = landed.shape[0]
        per_step = fetched_ref.shape[0]
        for i in range(per_step):
            at = position_ref[jnp.maximum(step - strips, 0) * per_step + i]
            fetched_ref[i] = landed[jnp.where(at < total, at, 0)]


def context_and_regions(
    position, sources, image, around, gain, qkv_weight, lce_weight, side, margin, evens_of, place_of
):
    height, width, channels = image.shape
    border = around[-1].shape[1]
    tokens = height * width
    strips = height // side
    pairs = position.shape[0]
    rounds = math.gcd(pairs, 4)
    tile = sources[0][0].shape[1:]
    full = lambda a: pl.BlockSpec(a.shape, lambda i, _: (0,) * a.ndim)
    operands = (image, *around, gain.reshape(1, channels), qkv_weight, lce_weight)
    flat = sum(sources, [])
    strip = pl.BlockSpec((side * width, channels), lambda i, _: (jnp.minimum(i, strips - 1), 0))
    return pl.pallas_call(
        functools.partial(
            context_kernel, side, margin, evens_of, place_of, tuple(map(len, sources))
        ),
        grid_spec=pltpu.PrefetchScalarGridSpec(
            num_scalar_prefetch=1,
            grid=(strips + rounds,),
            in_specs=[full(a) for a in operands]
            + [pl.BlockSpec(memory_space=pl.ANY)] * len(flat),
            out_specs=[
                strip,
                strip,
                pl.BlockSpec(
                    (pairs // rounds, *tile), lambda i, _: (jnp.maximum(i - strips, 0), 0, 0)
                ),
            ],
            scratch_shapes=[
                pltpu.VMEM((height + 2 * margin, width + 2 * border, channels), F32),
                pltpu.VMEM((rows_of(sources), *tile), BF16),
                pltpu.SemaphoreType.DMA((len(sources),)),
            ],
        ),
        out_shape=[
            jax.ShapeDtypeStruct((tokens, channels), F32),
            jax.ShapeDtypeStruct((tokens, channels), BF16),
            jax.ShapeDtypeStruct((pairs, *tile), BF16),
        ],
        cost_estimate=pl.CostEstimate(
            flops=tokens * channels * 600, bytes_accessed=40 * tokens * channels, transcendentals=0
        ),
        name="context",
    )(position, *operands, *flat)


def project(fetched, weight_ref):
    channels = fetched.shape[-1]
    projected = jnp.dot(
        fetched, weight_ref[:, channels : 3 * channels], preferred_element_type=F32
    ).astype(BF16)
    return projected[:, :channels], projected[:, channels:]


def score(queries, keys):
    area, channels = queries.shape
    lane = lax.broadcasted_iota(jnp.int32, (area, channels), 1) // (channels // HEADS)
    zero = jnp.zeros_like(queries)
    stacked = jnp.concatenate(
        [jnp.where(lane == head, queries, zero) for head in range(HEADS)], axis=0
    )
    return lax.dot_general(
        stacked, keys, (((1,), (1,)), ((), ())), preferred_element_type=F32
    )


def blend(weights, values):
    area, channels = weights.shape[0] // HEADS, values.shape[1]
    blended = jnp.dot(weights, values, preferred_element_type=F32)
    lane = lax.broadcasted_iota(jnp.int32, (area, channels), 1) // (channels // HEADS)
    picked = blended[:area]
    for head in range(1, HEADS):
        picked = jnp.where(lane == head, blended[head * area : (head + 1) * area], picked)
    return picked


def gelu(lifted):
    inner = lifted * (0.7978845608028654 + 0.035677408136300125 * (lifted * lifted))
    return lifted * (0.5 + 0.5 * jnp.tanh(inner))


def tail_kernel(
    side,
    picks,
    batch,
    early,
    late_count,
    position_ref,
    *refs,
):
    late_refs = refs[:late_count]
    (
    fetched_ref,
    query_ref,
    context_ref,
    image_ref,
    qkv_ref,
    out_weight_ref,
    gain_ref,
    up_ref,
    down_ref,
    result_ref,
    late_ref,
    combined_ref,
    ) = refs[late_count:]
    step = pl.program_id(0)
    last = pl.num_programs(0) - 2

    @pl.when(step == 0)
    def _():
        start = 0
        for part in late_refs:
            late_ref[pl.ds(start, part.shape[0])] = part[...]
            start += part.shape[0]

    area, channels = fetched_ref.shape[1:]
    exponent = (channels // HEADS) ** (-0.5) * math.log2(math.e)
    first = jnp.minimum(step, last) * (batch * picks)

    def piece(which):
        at = position_ref[first + which]
        is_late = at >= early
        return jnp.where(is_late, late_ref[jnp.where(is_late, at - early, 0)], fetched_ref[which])

    chunk = PAIR * area

    def attention(region):
        rows = pl.ds(region * area, area)
        fetched = jnp.concatenate(
            [piece(which) for which in range(region * picks, (region + 1) * picks)], axis=0
        )
        keys, values = project(fetched, qkv_ref)
        yield True
        scores = score(query_ref[rows, :], keys)
        yield True
        highest = jnp.max(scores, axis=-1, keepdims=True)
        expons = jnp.exp2((scores - highest) * exponent)
        yield True
        total = jnp.sum(expons, axis=-1, keepdims=True)
        weights = (expons * (1.0 / total)).astype(BF16)
        yield True
        attended = blend(weights, values)
        combined_ref[rows, :] = (attended + context_ref[rows, :]).astype(BF16)
        yield True

    def feed_forward(part):
        columns = pl.ds(part * PAIR * side, PAIR * side)
        image = regions_of(image_ref[:, columns, :].astype(F32), side)
        combined = combined_ref[pl.ds(part * chunk, chunk), :]
        residual = image + jnp.dot(combined, out_weight_ref[...], preferred_element_type=F32)
        yield True
        stored = residual.astype(BF16).astype(F32)
        second = normalize(stored, gain_ref[...]).astype(BF16)
        yield True
        lifted = jnp.dot(second, up_ref[...], preferred_element_type=F32)
        yield True
        hidden = gelu(lifted).astype(BF16)
        yield True
        refined = stored + jnp.dot(hidden, down_ref[...], preferred_element_type=F32)
        result_ref[:, columns, :] = strip_of(refined, side, PAIR * side).astype(BF16)
        yield True

    def run(forward, attend):
        lines = [feed_forward(part) for part in range(batch // PAIR)] if forward else []
        lines += [attention(region) for region in range(batch)] if attend else []
        while lines:
            lines = [line for line in lines if next(line, None) is not None]

    pl.when(step == 0)(lambda: run(False, True))
    pl.when((step > 0) & (step <= last))(lambda: run(True, True))
    pl.when(step > last)(lambda: run(True, False))


def tail(position, early, fetched, late, queries, context, image, weights, side, picks):
    height, width, channels = image.shape
    area = side * side
    per_row = width // side
    batch = math.gcd(per_row, 4)
    halves = per_row // batch
    steps = height // side * halves
    full = lambda a: pl.BlockSpec(a.shape, lambda i, position: (0,) * a.ndim)
    now = lambda i: jnp.minimum(i, steps - 1)
    before = lambda i: jnp.maximum(i - 1, 0)
    tokens = pl.BlockSpec((batch * area, channels), lambda i, position: (now(i), 0))
    strip = pl.BlockSpec(
        (side, batch * side, channels),
        lambda i, position: (before(i) // halves, before(i) % halves, 0),
    )
    regions = pl.BlockSpec((batch * picks, area, channels), lambda i, position: (now(i), 0, 0))
    return pl.pallas_call(
        functools.partial(tail_kernel, side, picks, batch, early, len(late)),
        grid_spec=pltpu.PrefetchScalarGridSpec(
            num_scalar_prefetch=1,
            grid=(steps + 1,),
            in_specs=[pl.BlockSpec(memory_space=pltpu.VMEM)] * len(late)
            + [regions, tokens, tokens, strip]
            + [full(w) for w in weights],
            out_specs=strip,
            scratch_shapes=[
                pltpu.VMEM((sum(part.shape[0] for part in late), area, channels), BF16),
                pltpu.VMEM((batch * area, channels), BF16),
            ],
        ),
        out_shape=jax.ShapeDtypeStruct(image.shape, BF16),
        cost_estimate=pl.CostEstimate(
            flops=image.size * 4000, bytes_accessed=16 * image.size, transcendentals=40 * image.size
        ),
        name="tail",
    )(position, *late, fetched, queries, context, image, *weights)


def layer_blocks(block, layers):
    if layers != 4:
        return [[block]] + [
            [lax.ppermute(block, "z", [(i, i ^ step) for i in range(layers)])]
            for step in range(1, layers)
        ]

    def hop(block, pairs):
        return lax.ppermute(block, "z", pairs)

    beside = hop(block, [(0, 1), (1, 0), (2, 3), (3, 2)])
    middle = hop(block, [(1, 2), (2, 1)])
    middle_two = hop(beside, [(1, 2), (2, 1)])
    ends_two = hop(middle, [(1, 0), (2, 3)])
    ends_three = hop(middle_two, [(1, 0), (2, 3)])
    return [[block], [beside], [middle_two, ends_two], [middle, ends_three]]


def block(
    image, routes, norm_gain, qkv_weight, lce_weight, out_weight, mlp_gain, up_weight, down_weight
):
    height, _, channels = image.shape
    layers, across = lax.axis_size("z"), lax.axis_size("x")
    peers = lax.axis_size("rows") * across
    devices = peers * layers
    region_rows, region_cols, pick_count = routes.shape
    side = height // region_rows
    pair_count = region_rows * region_cols * pick_count
    capacity = max(2, 2 * pair_count // devices)
    all_cols = region_cols * layers * across

    def place_of():
        return lax.axis_index("rows") * across + lax.axis_index("x"), lax.axis_index("z")

    def evens_of():
        return lax.axis_index("rows") % 2 == 0, lax.axis_index("x") % 2 == 0

    peer, layer = place_of()

    targets = routes.reshape(pair_count)
    target_row = targets // all_cols
    target_col = targets % all_cols
    owner_col = target_col // region_cols
    owner_layer = owner_col // across
    owner_peer = target_row // region_rows * across + owner_col % across
    local_index = target_row % region_rows * region_cols + target_col % region_cols
    owners = owner_peer * layers + owner_layer
    pairs = jnp.arange(pair_count, dtype=jnp.int32)
    earlier = (owners[:, None] == owners[None, :]) & (pairs[None, :] < pairs[:, None])
    slot = jnp.sum(earlier.astype(jnp.int32), axis=1)
    distance = owner_peer ^ peer
    step = owner_layer ^ layer
    whole, twin = (1, peers // 2), across
    lanes = -(-(layers + len(whole)) * capacity // 128) * 128
    asked = owner_peer * lanes + owner_layer * capacity + slot
    for number, far in enumerate(whole):
        through = (peer ^ twin) * lanes + (layers + number) * capacity + slot
        asked = jnp.where((step == 0) & (distance == far ^ twin), through, asked)
    slots = jnp.arange(peers * lanes, dtype=jnp.int32)
    requests = jnp.sum(
        jnp.where(asked[None, :] == slots[:, None], local_index[None, :], 0), axis=1
    )
    wanted = lax.all_to_all(
        requests.reshape(peers, 1, lanes), ("rows", "x"), 0, 0, tiled=True
    )

    margin = (lce_weight.shape[0] - 1) // 2
    normed, *edges = norm_regions(image, norm_gain, side, margin, 8, evens_of)

    def swap(part, far):
        return lax.ppermute(part, ("rows", "x"), [(i, i ^ far) for i in range(peers)])

    held = layer_blocks(normed, layers)
    given = [swap(normed, far) for far in whole]
    near_rows = with_pairs(edges[:2], "rows", lax.axis_size("rows"))

    tile = normed.shape[1:]
    position, total = jnp.zeros_like(slot), 0
    arrived = []

    def landing(options, *places):
        nonlocal position, total
        for condition, index in places:
            position = jnp.where(condition, total + index, position)
        total += options[0].shape[0]
        arrived[-1].append(options)

    relayed = [twin, *(far ^ twin for far in whole)]
    direct = [far for far in range(1, peers) if far not in relayed and far not in whole]
    jobs = [(0, 0, 0, twin, 0)]
    jobs += [(0, 1 + i, 1 + i, twin, layers + i) for i in range(len(whole))]
    jobs += [(1 + i, 0, 0, far, 0) for i, far in enumerate(direct)]
    jobs += [(1 + len(direct), None, 1 + len(whole), far, 1) for far in range(1, peers)]
    shapes = [(len(relayed) * capacity, *tile)] + [(capacity, *tile)] * len(direct)
    shapes += [(peers, capacity, *tile)]
    sources = [[normed], *([part] for part in given), held[1]]
    *parts, joint, paired, other = pack(
        jobs,
        shapes,
        sources,
        place_of,
        wanted,
        capacity,
        layers,
        (*near_rows, *edges[2:]),
        evens_of,
    )
    got = [swap(part, far) for part, far in zip(parts, [twin, *direct])]
    joint = lax.all_to_all(joint, ("rows", "x"), 0, 0, tiled=True)
    around = (*near_rows, *with_pairs((paired, other), ("z", "x"), layers * across))
    arrived.append([])
    landing([normed], ((step == 0) & (distance == 0), local_index))
    for far, part in zip(whole, given):
        landing([part], ((step == 0) & (distance == far), local_index))
    landing(
        [got[0]],
        *(
            ((step == 0) & (distance == far), i * capacity + slot)
            for i, far in enumerate(relayed)
        ),
    )
    for far, part in zip(direct, got[1:]):
        landing([part], ((step == 0) & (distance == far), slot))
    landing(held[1], ((step == 1) & (distance == 0), local_index))
    landing(
        [joint.reshape(-1, *tile)],
        ((step == 1) & (distance != 0), owner_peer * capacity + slot),
    )

    for chunk in range(2, layers):
        last = chunk == layers - 1
        jobs = [(far - 1, 0, 0, far, chunk) for far in range(1, peers)]
        shapes = [(capacity, *tile)] * (peers - 1)
        parts = pack(jobs, shapes, [held[chunk]], place_of, wanted, capacity, layers)
        got = [swap(part, far) for far, part in enumerate(parts, 1)]
        landing(held[chunk], ((step == chunk) & (distance == 0), local_index))
        if last:
            early = total
            arrived.append([])
        for far, part in enumerate(got, 1):
            landing([part], ((step == chunk) & (distance == far), slot))
    late = sum(arrived.pop(), [])
    context, queries, fetched = context_and_regions(
        position,
        sum(arrived, []),
        image,
        around,
        norm_gain,
        qkv_weight,
        lce_weight,
        side,
        margin,
        evens_of,
        place_of,
    )
    weights = (
        qkv_weight,
        out_weight,
        mlp_gain.reshape(1, channels),
        up_weight,
        down_weight,
    )
    return tail(position, early, fetched, late, queries, context, image, weights, side, pick_count)


def solution(mesh):
    devices = mesh.devices
    layers = len({device.coords[2] for device in devices[0]})
    split = Mesh(
        devices.reshape(devices.shape[0], layers, devices.shape[1] // layers), ("rows", "z", "x")
    )
    grid = P("rows", ("z", "x"), None)
    in_specs = (grid, grid, P(), P(), P(), P(), P(), P(), P())
    return jax.shard_map(block, mesh=split, in_specs=in_specs, out_specs=grid, check_vma=False)
```

```python
import functools
import math

import jax
import jax.numpy as jnp
from jax import lax
from jax.experimental import pallas as pl
from jax.experimental.pallas import tpu as pltpu
from jax.sharding import Mesh
from jax.sharding import PartitionSpec as P

HEADS = 4
PAIR = 4
EPSILON = 1e-06
F32 = jnp.float32
BF16 = jnp.bfloat16


def with_pairs(parts, axis, count):
    links = ([], [])
    for i in range(count - 1):
        links[i % 2].extend([(i, i + 1), (i + 1, i)])
    return [lax.ppermute(part, axis, pairs) for part, pairs in zip(parts, links)]


def either(flag, yes, no):
    return jnp.where(flag, yes, no)


def normalize(floats, gain):
    centered = floats - jnp.mean(floats, axis=-1, keepdims=True)
    spread = jnp.mean(centered * centered, axis=-1, keepdims=True)
    return centered * lax.rsqrt(spread + EPSILON) * gain


def regions_of(strip, side):
    height, width, channels = strip.shape
    return (
        strip.reshape(height, width // side, side, channels)
        .transpose(1, 0, 2, 3)
        .reshape(height * width, channels)
    )


def strip_of(tokens, side, width):
    channels = tokens.shape[-1]
    return (
        tokens.reshape(width // side, side, side, channels)
        .transpose(1, 0, 2, 3)
        .reshape(side, width, channels)
    )


def norm_kernel(side, evens_of, image_ref, gain_ref, out_ref, *edge_refs):
    step = pl.program_id(0)
    *row_refs, left_ref, right_ref = edge_refs
    tokens = image_ref[...].astype(F32)
    normed = normalize(tokens, gain_ref[...])
    out_ref[...] = regions_of(normed, side).astype(BF16).reshape(out_ref.shape)
    margin, width, border = row_refs[0].shape[0], tokens.shape[1], left_ref.shape[1]
    left_ref[...] = tokens[:, :border].astype(BF16)
    right_ref[...] = tokens[:, width - border :].astype(BF16)
    row_even = evens_of()[0]

    def put(even, odd, first):
        def store(ref):
            ref[...] = image_ref[pl.ds(first, margin)]

        pl.when(row_even)(lambda: store(row_refs[even]))
        pl.when(~row_even)(lambda: store(row_refs[odd]))

    pl.when(step == 0)(lambda: put(1, 0, 0))
    pl.when(step == pl.num_programs(0) - 1)(lambda: put(0, 1, side - margin))


def norm_regions(image, gain, side, margin, border, evens_of):
    height, width, channels = image.shape
    per_row = width // side
    edge = jax.ShapeDtypeStruct((margin, width, channels), BF16)
    flank = jax.ShapeDtypeStruct((height, border, channels), BF16)
    return pl.pallas_call(
        functools.partial(norm_kernel, side, evens_of),
        grid=(height // side,),
        in_specs=[
            pl.BlockSpec((side, width, channels), lambda i: (i, 0, 0)),
            pl.BlockSpec((1, channels), lambda i: (0, 0)),
        ],
        out_specs=[
            pl.BlockSpec((per_row, side * side, channels), lambda i: (i, 0, 0)),
            pl.BlockSpec(edge.shape, lambda i: (0, 0, 0)),
            pl.BlockSpec(edge.shape, lambda i: (0, 0, 0)),
            pl.BlockSpec((side, border, channels), lambda i: (i, 0, 0)),
            pl.BlockSpec((side, border, channels), lambda i: (i, 0, 0)),
        ],
        out_shape=[
            jax.ShapeDtypeStruct((height // side * per_row, side * side, channels), BF16),
            edge,
            edge,
            flank,
            flank,
        ],
        cost_estimate=pl.CostEstimate(
            flops=10 * image.size, bytes_accessed=4 * image.size, transcendentals=0
        ),
        name="norm_regions",
    )(image, gain.reshape(1, channels))


def is_inside(layer):
    return (layer == 1) | (layer == 2)


def frame_kernel(evens, row_refs, flank_refs, out_refs):
    row_even, col_even = evens
    margin, width = row_refs[0].shape[:2]
    height, border = flank_refs[0].shape[:2]
    paired, other = row_refs[0][...].astype(F32), row_refs[1][...].astype(F32)
    above, below = either(row_even, other, paired), either(row_even, paired, other)
    for out_ref, flag in ((out_refs[0], col_even), (out_refs[1], ~col_even)):
        right = lambda rows: rows[:, width - border :]
        left = lambda rows: rows[:, :border]
        out_ref[pl.ds(0, margin)] = either(flag, right(above), left(above)).astype(BF16)
        out_ref[pl.ds(margin, height)] = either(flag, flank_refs[1][...], flank_refs[0][...])
        out_ref[pl.ds(margin + height, margin)] = either(flag, right(below), left(below)).astype(
            BF16
        )


def pack_kernel(jobs, options, outputs, evens_of, capacity, layers, place_of, wanted_ref, *refs):
    peer, layer = place_of()
    sources = refs[: sum(options)]
    outs = refs[len(refs) - outputs :]
    if evens_of is not None:
        edges = refs[sum(options) : sum(options) + 4]
        frame_kernel(evens_of(), edges[:2], edges[2:], outs[-2:])
    inside = is_inside(layer)

    def fill(source_ref, out_ref, place, distance, column):
        other = peer ^ distance
        base = ((layer ^ column) if column < layers else column) * capacity
        for slot in range(capacity):
            region = source_ref[wanted_ref[other, 0, base + slot]]
            if place is None:
                out_ref[other, slot] = region
            else:
                out_ref[place * capacity + slot] = region

    def fill_all(shift, chosen):
        for out, place, source, distance, column in chosen:
            at = sum(options[:source]) + shift
            fill(sources[at], outs[out], place, distance, column)

    fill_all(0, [job for job in jobs if options[job[2]] == 1])
    paired = [job for job in jobs if options[job[2]] == 2]
    if paired:
        pl.when(inside)(functools.partial(fill_all, 0, paired))
        pl.when(~inside)(functools.partial(fill_all, 1, paired))


def pack(jobs, shapes, sources, place_of, wanted, capacity, layers, frame=(), evens_of=None):
    flat = sum(sources, [])
    if frame:
        margin, (height, border, channels) = frame[0].shape[0], frame[2].shape
        shapes = shapes + [(height + 2 * margin, border, channels)] * 2
    in_vmem = pl.BlockSpec(memory_space=pltpu.VMEM)
    return pl.pallas_call(
        functools.partial(
            pack_kernel,
            tuple(jobs),
            tuple(map(len, sources)),
            len(shapes),
            evens_of,
            capacity,
            layers,
            place_of,
        ),
        in_specs=[pl.BlockSpec(memory_space=pltpu.SMEM)] + [in_vmem] * (len(flat) + len(frame)),
        out_specs=[in_vmem] * len(shapes),
        out_shape=[jax.ShapeDtypeStruct(a, BF16) for a in shapes],
        cost_estimate=pl.CostEstimate(
            flops=0, bytes_accessed=4 * sum(map(math.prod, shapes)), transcendentals=0
        ),
        name="pack",
    )(wanted, *flat, *frame)


def load_all(options, sources, landed, sems, layer, wait):
    start, at = 0, 0
    inside = is_inside(layer)
    for i, count in enumerate(options):
        size = sources[at].shape[0]
        copies = [
            pltpu.make_async_copy(source, landed.at[pl.ds(start, size)], sems.at[i])
            for source in sources[at : at + count]
        ]
        if wait:
            copies[0].wait()
        elif count == 1:
            copies[0].start()
        else:
            pl.when(inside)(copies[0].start)
            pl.when(~inside)(copies[1].start)
        start += size
        at += count


def rows_of(sources):
    return sum(options[0].shape[0] for options in sources)


def context_kernel(
    side,
    margin,
    evens_of,
    place_of,
    options,
    position_ref,
    image_ref,
    row_pair_ref,
    row_other_ref,
    col_pair_ref,
    col_other_ref,
    gain_ref,
    weight_ref,
    lce_ref,
    *refs,
):
    sources = refs[: sum(options)]
    context_ref, query_ref, fetched_ref, padded, landed, sems = refs[sum(options) :]
    step = pl.program_id(0)
    height, width, channels = image_ref.shape
    strips = height // side
    beside, border = col_pair_ref.shape[1], 8

    @pl.when(step == 0)
    def _():
        load_all(options, sources, landed, sems, place_of()[1], False)
        row_even, col_even = evens_of()
        inner = pl.ds(border, width)
        paired, other = row_pair_ref[...].astype(F32), row_other_ref[...].astype(F32)
        padded[:margin, inner] = either(row_even, other, paired)
        padded[pl.ds(margin, height), inner] = image_ref[...].astype(F32)
        padded[pl.ds(margin + height, margin), inner] = either(row_even, paired, other)
        paired, other = col_pair_ref[...].astype(F32), col_other_ref[...].astype(F32)
        padded[:, pl.ds(border - beside, beside)] = either(col_even, other, paired)
        padded[:, pl.ds(border + width, beside)] = either(col_even, paired, other)

    @pl.when(step < strips)
    def _():
        rows = side + 2 * margin
        strip = padded[pl.ds(jnp.minimum(step, strips - 1) * side, rows)]
        wide = strip.shape[1]
        normed = normalize(strip, gain_ref[...]).astype(BF16).reshape(rows * wide, channels)
        weight = jnp.concatenate([weight_ref[:, :channels], weight_ref[:, 2 * channels :]], axis=1)
        projected = jnp.dot(normed, weight, preferred_element_type=F32).astype(BF16)
        values = projected[:, channels:].astype(F32).reshape(rows, wide, channels)
        summed = jnp.zeros((side, width, channels), F32)
        for col in range(2 * margin + 1):
            moved = pltpu.roll(values, wide - (border - margin + col), 1)[:, :width]
            for row in range(2 * margin + 1):
                summed = summed + moved[row : row + side] * lce_ref[row, pl.ds(col, 1), :]
        context_ref[...] = regions_of(summed, side)
        queries = projected[:, :channels].astype(F32).reshape(rows, wide, channels)
        inner = queries[margin : margin + side, border : border + width]
        query_ref[...] = regions_of(inner, side).astype(BF16)

    @pl.when(step == strips)
    def _():
        load_all(options, sources, landed, sems, place_of()[1], True)

    @pl.when(step >= strips)
    def _():
        total = landed.shape[0]
        per_step = fetched_ref.shape[0]
        for i in range(per_step):
            at = position_ref[jnp.maximum(step - strips, 0) * per_step + i]
            fetched_ref[i] = landed[jnp.where(at < total, at, 0)]


def context_and_regions(
    position, sources, image, around, gain, qkv_weight, lce_weight, side, margin, evens_of, place_of
):
    height, width, channels = image.shape
    border = 8
    tokens = height * width
    strips = height // side
    pairs = position.shape[0]
    rounds = math.gcd(pairs, 4)
    tile = sources[0][0].shape[1:]
    full = lambda a: pl.BlockSpec(a.shape, lambda i, _: (0,) * a.ndim)
    operands = (image, *around, gain.reshape(1, channels), qkv_weight, lce_weight)
    flat = sum(sources, [])
    strip = pl.BlockSpec((side * width, channels), lambda i, _: (jnp.minimum(i, strips - 1), 0))
    return pl.pallas_call(
        functools.partial(
            context_kernel, side, margin, evens_of, place_of, tuple(map(len, sources))
        ),
        grid_spec=pltpu.PrefetchScalarGridSpec(
            num_scalar_prefetch=1,
            grid=(strips + rounds,),
            in_specs=[full(a) for a in operands]
            + [pl.BlockSpec(memory_space=pl.ANY)] * len(flat),
            out_specs=[
                strip,
                strip,
                pl.BlockSpec(
                    (pairs // rounds, *tile), lambda i, _: (jnp.maximum(i - strips, 0), 0, 0)
                ),
            ],
            scratch_shapes=[
                pltpu.VMEM((height + 2 * margin, width + 2 * border, channels), F32),
                pltpu.VMEM((rows_of(sources), *tile), BF16),
                pltpu.SemaphoreType.DMA((len(sources),)),
            ],
        ),
        out_shape=[
            jax.ShapeDtypeStruct((tokens, channels), F32),
            jax.ShapeDtypeStruct((tokens, channels), BF16),
            jax.ShapeDtypeStruct((pairs, *tile), BF16),
        ],
        cost_estimate=pl.CostEstimate(
            flops=tokens * channels * 600, bytes_accessed=40 * tokens * channels, transcendentals=0
        ),
        name="context",
    )(position, *operands, *flat)


def project(fetched, weight_ref):
    channels = fetched.shape[-1]
    projected = jnp.dot(
        fetched, weight_ref[:, channels : 3 * channels], preferred_element_type=F32
    ).astype(BF16)
    return projected[:, :channels], projected[:, channels:]


def score(queries, keys):
    area, channels = queries.shape
    lane = lax.broadcasted_iota(jnp.int32, (area, channels), 1) // (channels // HEADS)
    zero = jnp.zeros_like(queries)
    stacked = jnp.concatenate(
        [jnp.where(lane == head, queries, zero) for head in range(HEADS)], axis=0
    )
    return lax.dot_general(
        stacked, keys, (((1,), (1,)), ((), ())), preferred_element_type=F32
    )


def blend(weights, values):
    area, channels = weights.shape[0] // HEADS, values.shape[1]
    blended = jnp.dot(weights, values, preferred_element_type=F32)
    lane = lax.broadcasted_iota(jnp.int32, (area, channels), 1) // (channels // HEADS)
    picked = blended[:area]
    for head in range(1, HEADS):
        picked = jnp.where(lane == head, blended[head * area : (head + 1) * area], picked)
    return picked


def gelu(lifted):
    inner = lifted * (0.7978845608028654 + 0.035677408136300125 * (lifted * lifted))
    return lifted * (0.5 + 0.5 * jnp.tanh(inner))


def tail_kernel(
    side,
    picks,
    batch,
    early,
    late_count,
    position_ref,
    *refs,
):
    late_refs = refs[:late_count]
    (
    fetched_ref,
    query_ref,
    context_ref,
    image_ref,
    qkv_ref,
    out_weight_ref,
    gain_ref,
    up_ref,
    down_ref,
    result_ref,
    late_ref,
    combined_ref,
    ) = refs[late_count:]
    step = pl.program_id(0)
    last = pl.num_programs(0) - 2

    @pl.when(step == 0)
    def _():
        start = 0
        for part in late_refs:
            late_ref[pl.ds(start, part.shape[0])] = part[...]
            start += part.shape[0]

    area, channels = fetched_ref.shape[1:]
    exponent = (channels // HEADS) ** (-0.5) * math.log2(math.e)
    first = jnp.minimum(step, last) * (batch * picks)

    def piece(which):
        at = position_ref[first + which]
        is_late = at >= early
        return jnp.where(is_late, late_ref[jnp.where(is_late, at - early, 0)], fetched_ref[which])

    chunk = PAIR * area

    def attention(region):
        rows = pl.ds(region * area, area)
        fetched = jnp.concatenate(
            [piece(which) for which in range(region * picks, (region + 1) * picks)], axis=0
        )
        keys, values = project(fetched, qkv_ref)
        yield True
        scores = score(query_ref[rows, :], keys)
        yield True
        highest = jnp.max(scores, axis=-1, keepdims=True)
        expons = jnp.exp2((scores - highest) * exponent)
        yield True
        total = jnp.sum(expons, axis=-1, keepdims=True)
        weights = (expons * (1.0 / total)).astype(BF16)
        yield True
        attended = blend(weights, values)
        combined_ref[rows, :] = (attended + context_ref[rows, :]).astype(BF16)
        yield True

    def feed_forward(part):
        columns = pl.ds(part * PAIR * side, PAIR * side)
        image = regions_of(image_ref[:, columns, :].astype(F32), side)
        combined = combined_ref[pl.ds(part * chunk, chunk), :]
        residual = image + jnp.dot(combined, out_weight_ref[...], preferred_element_type=F32)
        yield True
        stored = residual.astype(BF16).astype(F32)
        second = normalize(stored, gain_ref[...]).astype(BF16)
        yield True
        lifted = jnp.dot(second, up_ref[...], preferred_element_type=F32)
        yield True
        hidden = gelu(lifted).astype(BF16)
        yield True
        refined = stored + jnp.dot(hidden, down_ref[...], preferred_element_type=F32)
        result_ref[:, columns, :] = strip_of(refined, side, PAIR * side).astype(BF16)
        yield True

    def run(forward, attend):
        lines = [feed_forward(part) for part in range(batch // PAIR)] if forward else []
        lines += [attention(region) for region in range(batch)] if attend else []
        while lines:
            lines = [line for line in lines if next(line, None) is not None]

    pl.when(step == 0)(lambda: run(False, True))
    pl.when((step > 0) & (step <= last))(lambda: run(True, True))
    pl.when(step > last)(lambda: run(True, False))


def tail(position, early, fetched, late, queries, context, image, weights, side, picks):
    height, width, channels = image.shape
    area = side * side
    per_row = width // side
    batch = math.gcd(per_row, 8)
    halves = per_row // batch
    steps = height // side * halves
    full = lambda a: pl.BlockSpec(a.shape, lambda i, position: (0,) * a.ndim)
    now = lambda i: jnp.minimum(i, steps - 1)
    before = lambda i: jnp.maximum(i - 1, 0)
    tokens = pl.BlockSpec((batch * area, channels), lambda i, position: (now(i), 0))
    strip = pl.BlockSpec(
        (side, batch * side, channels),
        lambda i, position: (before(i) // halves, before(i) % halves, 0),
    )
    regions = pl.BlockSpec((batch * picks, area, channels), lambda i, position: (now(i), 0, 0))
    return pl.pallas_call(
        functools.partial(tail_kernel, side, picks, batch, early, len(late)),
        grid_spec=pltpu.PrefetchScalarGridSpec(
            num_scalar_prefetch=1,
            grid=(steps + 1,),
            in_specs=[pl.BlockSpec(memory_space=pltpu.VMEM)] * len(late)
            + [regions, tokens, tokens, strip]
            + [full(w) for w in weights],
            out_specs=strip,
            scratch_shapes=[
                pltpu.VMEM((sum(part.shape[0] for part in late), area, channels), BF16),
                pltpu.VMEM((batch * area, channels), BF16),
            ],
        ),
        out_shape=jax.ShapeDtypeStruct(image.shape, BF16),
        cost_estimate=pl.CostEstimate(
            flops=image.size * 4000, bytes_accessed=16 * image.size, transcendentals=40 * image.size
        ),
        name="tail",
    )(position, *late, fetched, queries, context, image, *weights)


def layer_blocks(block, layers):
    if layers != 4:
        return [[block]] + [
            [lax.ppermute(block, "z", [(i, i ^ step) for i in range(layers)])]
            for step in range(1, layers)
        ]

    def hop(block, pairs):
        return lax.ppermute(block, "z", pairs)

    beside = hop(block, [(0, 1), (1, 0), (2, 3), (3, 2)])
    middle = hop(block, [(1, 2), (2, 1)])
    middle_two = hop(beside, [(1, 2), (2, 1)])
    ends_two = hop(middle, [(1, 0), (2, 3)])
    ends_three = hop(middle_two, [(1, 0), (2, 3)])
    return [[block], [beside], [middle_two, ends_two], [middle, ends_three]]


def block(
    image, routes, norm_gain, qkv_weight, lce_weight, out_weight, mlp_gain, up_weight, down_weight
):
    height, _, channels = image.shape
    layers, across = lax.axis_size("z"), lax.axis_size("x")
    peers = lax.axis_size("rows") * across
    devices = peers * layers
    region_rows, region_cols, pick_count = routes.shape
    side = height // region_rows
    pair_count = region_rows * region_cols * pick_count
    capacity = max(2, 2 * pair_count // devices)
    all_cols = region_cols * layers * across

    def place_of():
        return lax.axis_index("rows") * across + lax.axis_index("x"), lax.axis_index("z")

    def evens_of():
        return lax.axis_index("rows") % 2 == 0, lax.axis_index("x") % 2 == 0

    peer, layer = place_of()

    targets = routes.reshape(pair_count)
    target_row = targets // all_cols
    target_col = targets % all_cols
    owner_col = target_col // region_cols
    owner_layer = owner_col // across
    owner_peer = target_row // region_rows * across + owner_col % across
    local_index = target_row % region_rows * region_cols + target_col % region_cols
    owners = owner_peer * layers + owner_layer
    pairs = jnp.arange(pair_count, dtype=jnp.int32)
    earlier = (owners[:, None] == owners[None, :]) & (pairs[None, :] < pairs[:, None])
    slot = jnp.sum(earlier.astype(jnp.int32), axis=1)
    distance = owner_peer ^ peer
    step = owner_layer ^ layer
    whole, twin = (1, peers // 2), across
    lanes = -(-(layers + len(whole)) * capacity // 128) * 128
    asked = owner_peer * lanes + owner_layer * capacity + slot
    for number, far in enumerate(whole):
        through = (peer ^ twin) * lanes + (layers + number) * capacity + slot
        asked = jnp.where((step == 0) & (distance == far ^ twin), through, asked)
    slots = jnp.arange(peers * lanes, dtype=jnp.int32)
    requests = jnp.sum(
        jnp.where(asked[None, :] == slots[:, None], local_index[None, :], 0), axis=1
    )
    wanted = lax.all_to_all(
        requests.reshape(peers, 1, lanes), ("rows", "x"), 0, 0, tiled=True
    )

    margin = (lce_weight.shape[0] - 1) // 2
    normed, *edges = norm_regions(image, norm_gain, side, margin, margin, evens_of)

    def swap(part, far):
        return lax.ppermute(part, ("rows", "x"), [(i, i ^ far) for i in range(peers)])

    held = layer_blocks(normed, layers)
    given = [swap(normed, far) for far in whole]
    near_rows = with_pairs(edges[:2], "rows", lax.axis_size("rows"))

    tile = normed.shape[1:]
    position, total = jnp.zeros_like(slot), 0
    arrived = []

    def landing(options, *places):
        nonlocal position, total
        for condition, index in places:
            position = jnp.where(condition, total + index, position)
        total += options[0].shape[0]
        arrived[-1].append(options)

    relayed = [twin, *(far ^ twin for far in whole)]
    direct = [far for far in range(1, peers) if far not in relayed and far not in whole]
    jobs = [(0, 0, 0, twin, 0)]
    jobs += [(0, 1 + i, 1 + i, twin, layers + i) for i in range(len(whole))]
    jobs += [(1 + i, 0, 0, far, 0) for i, far in enumerate(direct)]
    jobs += [(1 + len(direct), None, 1 + len(whole), far, 1) for far in range(1, peers)]
    shapes = [(len(relayed) * capacity, *tile)] + [(capacity, *tile)] * len(direct)
    shapes += [(peers, capacity, *tile)]
    sources = [[normed], *([part] for part in given), held[1]]
    *parts, joint, paired, other = pack(
        jobs,
        shapes,
        sources,
        place_of,
        wanted,
        capacity,
        layers,
        (*near_rows, *edges[2:]),
        evens_of,
    )
    got = [swap(part, far) for part, far in zip(parts, [twin, *direct])]
    joint = lax.all_to_all(joint, ("rows", "x"), 0, 0, tiled=True)
    around = (*near_rows, *with_pairs((paired, other), ("z", "x"), layers * across))
    arrived.append([])
    landing([normed], ((step == 0) & (distance == 0), local_index))
    for far, part in zip(whole, given):
        landing([part], ((step == 0) & (distance == far), local_index))
    landing(
        [got[0]],
        *(
            ((step == 0) & (distance == far), i * capacity + slot)
            for i, far in enumerate(relayed)
        ),
    )
    for far, part in zip(direct, got[1:]):
        landing([part], ((step == 0) & (distance == far), slot))
    landing(held[1], ((step == 1) & (distance == 0), local_index))
    landing(
        [joint.reshape(-1, *tile)],
        ((step == 1) & (distance != 0), owner_peer * capacity + slot),
    )

    for chunk in range(2, layers):
        last = chunk == layers - 1
        jobs = [(far - 1, 0, 0, far, chunk) for far in range(1, peers)]
        shapes = [(capacity, *tile)] * (peers - 1)
        parts = pack(jobs, shapes, [held[chunk]], place_of, wanted, capacity, layers)
        got = [swap(part, far) for far, part in enumerate(parts, 1)]
        landing(held[chunk], ((step == chunk) & (distance == 0), local_index))
        if last:
            early = total
            arrived.append([])
        for far, part in enumerate(got, 1):
            landing([part], ((step == chunk) & (distance == far), slot))
    late = sum(arrived.pop(), [])
    context, queries, fetched = context_and_regions(
        position,
        sum(arrived, []),
        image,
        around,
        norm_gain,
        qkv_weight,
        lce_weight,
        side,
        margin,
        evens_of,
        place_of,
    )
    weights = (
        qkv_weight,
        out_weight,
        mlp_gain.reshape(1, channels),
        up_weight,
        down_weight,
    )
    return tail(position, early, fetched, late, queries, context, image, weights, side, pick_count)


def solution(mesh):
    devices = mesh.devices
    layers = len({device.coords[2] for device in devices[0]})
    split = Mesh(
        devices.reshape(devices.shape[0], layers, devices.shape[1] // layers), ("rows", "z", "x")
    )
    grid = P("rows", ("z", "x"), None)
    in_specs = (grid, grid, P(), P(), P(), P(), P(), P(), P())
    return jax.shard_map(block, mesh=split, in_specs=in_specs, out_specs=grid, check_vma=False)
```
